32 devices in a mesh: pipe: 4 (over y, x), ctx: 8 (over z, core).
Axes of the slice: x: 2, y: 2, z: 4, core: 2. Of those that a mesh axis runs over, the one named last changes fastest.
Arguments:
- tokens: bfloat16 [4, 1024, 8192], P('pipe', 'ctx')
- queries: bfloat16 [4, 1024, 4096], P('pipe', 'ctx')
- key_weight: bfloat16 [8192, 512], P(('pipe', 'ctx'))
- value_weight: bfloat16 [8192, 512], P(('pipe', 'ctx')), may hold values from -0.0625 to 0.0625
- block_order: int32 [16], replicated, may hold values from 0 to 15, as said below
Outputs:
- attended: bfloat16 [4, 1024, 4096], P('pipe', 'ctx')
The draws below stay inside these ranges and needn't reach their ends.
Inputs may be any that keep to these rules, and one draw needn't show every extreme that they name: `block_order`: each of the 16 half-blocks appears once.
All inputs are finite; a program needn't handle non-finite values.
Results may differ from the reference program's by a relative error of at most 0.0056.
The reference program's roundings to bfloat16 on the way count: a program that leaves them out, or rounds other values in their place, can miss the bound.
Values may be sent and summed in bfloat16 or wider, within the bound.
A program may use at most 64 MiB of HBM per device.

```python
import jax
import jax.numpy as jnp
from jax import lax

MODEL_WIDTH = 8192
QUERY_HEADS = 32
KEY_VALUE_HEADS = 4
HEAD_SIZE = 128
HALF = 64
HALVES = 16
SEQUENCE_TOKENS = 1024
MICRO = 4
QUERY_GROUP = 8
KVW = 512


def order_of(key):
    return jax.random.permutation(jax.random.fold_in(key, 11), HALVES).astype(jnp.int32)


def key_matrix(key):
    return jax.random.normal(jax.random.fold_in(key, 21), (MODEL_WIDTH, KEY_VALUE_HEADS * HEAD_SIZE), jnp.float32) * MODEL_WIDTH ** (-0.5)


def draw_block_order(key, part):
    return order_of(key)


def draw_key_weight(key, part):
    return key_matrix(key).astype(jnp.bfloat16)


def draw_tokens(key, part):
    base = jnp.clip(jax.random.normal(jax.random.fold_in(key, 41), (MICRO, SEQUENCE_TOKENS, MODEL_WIDTH), jnp.float32), -6.0, 6.0)
    return base.astype(jnp.bfloat16)


def draw_queries(key, part):
    base = jnp.clip(jax.random.normal(jax.random.fold_in(key, 43), (MICRO, SEQUENCE_TOKENS, QUERY_HEADS * HEAD_SIZE), jnp.float32), -6.0, 6.0)
    return base.astype(jnp.bfloat16)


def steps_of(own_key, shape, cuts, smallest, high):
    loudness = 1.0
    for axis_at, parts in cuts:
        steps = jax.random.uniform(jax.random.fold_in(jax.random.fold_in(own_key, 6), axis_at), (parts,), jnp.float32, smallest / len(cuts), high / len(cuts))
        loudness = loudness * jnp.repeat(jnp.exp(steps), shape[axis_at] // parts).reshape((-1,) + (1,) * (len(shape) - 1 - axis_at))
    return loudness


def scatter_about(rng, dims, width, reach, pieces=(), held_as=jnp.bfloat16):
    result = jax.random.normal(rng, dims, jnp.float32) * width
    if len(pieces) > 0:
        result = steps_of(rng, dims, pieces, -0.22, 0.18) * result
    return jnp.clip(result, min=-reach, max=reach).astype(held_as)


def setup_inputs(seed: int = 0) -> dict:
    arg_keys = jax.random.split(jax.random.key(seed), 6)
    tokens = draw_tokens(jax.random.fold_in(arg_keys[5], 71), 0)
    queries = draw_queries(jax.random.fold_in(arg_keys[5], 71), 0)
    key_weight = draw_key_weight(jax.random.fold_in(arg_keys[5], 71), 0)
    value_weight = scatter_about(arg_keys[3], (MODEL_WIDTH, KVW), MODEL_WIDTH ** -0.5, 0.0625, ((0, 32),))
    block_order = draw_block_order(jax.random.fold_in(arg_keys[5], 71), 0)
    return dict(tokens=tokens, queries=queries, key_weight=key_weight, value_weight=value_weight, block_order=block_order)


def reference(tokens, queries, key_weight, value_weight, block_order):
    position = jnp.repeat(block_order * HALF, HALF) + jnp.tile(jnp.arange(HALF, dtype=jnp.int32), HALVES)
    allowed = position[None, :] <= position[:, None]
    scale = 1.0 / (HEAD_SIZE ** 0.5)

    def one_batch(pair):
        hidden, query_rows = pair
        key_rows = jnp.dot(hidden, key_weight, preferred_element_type=jnp.float32).astype(jnp.bfloat16)
        value_rows = jnp.dot(hidden, value_weight, preferred_element_type=jnp.float32).astype(jnp.bfloat16)
        query_heads = query_rows.reshape(SEQUENCE_TOKENS, QUERY_HEADS, HEAD_SIZE).transpose(1, 0, 2)
        key_head_rows = jnp.repeat(key_rows.reshape(SEQUENCE_TOKENS, KEY_VALUE_HEADS, HEAD_SIZE).transpose(1, 0, 2), QUERY_GROUP, axis=0)
        value_head_rows = jnp.repeat(value_rows.reshape(SEQUENCE_TOKENS, KEY_VALUE_HEADS, HEAD_SIZE).transpose(1, 0, 2), QUERY_GROUP, axis=0)

        def one_head(triple):
            query_one, key_one, value_one = triple
            score = jnp.dot(query_one, key_one.T, preferred_element_type=jnp.float32) * scale
            largest = jnp.max(jnp.where(allowed, score, -jnp.inf), axis=1)
            expo = jnp.where(allowed, jnp.exp(score - largest[:, None]), 0.0)
            total = jnp.sum(expo, axis=1)
            weight = expo.astype(jnp.bfloat16)
            summed = jnp.dot(weight, value_one, preferred_element_type=jnp.float32)
            return (summed / total[:, None]).astype(jnp.bfloat16)

        heads_out = lax.map(one_head, (query_heads, key_head_rows, value_head_rows))
        return heads_out.transpose(1, 0, 2).reshape(SEQUENCE_TOKENS, QUERY_HEADS * HEAD_SIZE)

    return lax.map(one_batch, (tokens, queries))
```

```python
import functools

import jax
import jax.numpy as jnp
from jax import lax
from jax.experimental import pallas as pl
from jax.experimental.pallas import tpu as pltpu
from jax.sharding import PartitionSpec as P

HEAD_SIZE = 128
LOG2E = 1.4426950408889634
MESH = pl.DeviceIdType.MESH
PARTIAL = jnp.bfloat16
TOKEN_PARTS = 2
VMEM_LIMIT = 60 * 1024 * 1024


def block_at(index, size):
    return pl.ds(pl.multiple_of(index * size, size), size)


def remote(src, dst, send_sem, recv_sem, device_id):
    return pltpu.make_async_remote_copy(
        src_ref=src, dst_ref=dst, send_sem=send_sem, recv_sem=recv_sem, device_id=device_id, device_id_type=MESH
    )


def kernel(
    pipes, ctxs, half,
    tok, qry, kw, vw, order, out,
    wbuf, xbuf, pout, pin, mine, kvbuf, qbuf, cap, pbuf, abuf, obuf,
    w_send, w_recv, w_cross, kv_send, kv_recv, x_send, x_recv, xr_send, xr_recv, xo_send, xo_recv,
    p_send, p_recv, q_sem, o_local, o_send, o_recv, local,
):
    rows = 2 * xbuf.shape[3]
    small = xbuf.shape[3]
    slice_rows = xbuf.shape[4]
    parts = x_send.shape[2]
    part_rows = slice_rows // parts
    deep = kw.shape[0]
    lines = ctxs // 2
    heads = kw.shape[1] // HEAD_SIZE
    per = heads // 2
    pieces = 2 * per
    group = qbuf.shape[1] // (per * HEAD_SIZE)
    chip_rows = 2 * rows
    seq = ctxs * rows
    half_columns = qbuf.shape[1]
    pipe = lax.axis_index("pipe")
    me = lax.axis_index("ctx")
    line = me // 2
    core = me % 2
    partner = me + 1 - 2 * core


    def weight_source(j, to_core):
        return (kw, vw)[j // per].at[:, block_at(to_core * per + j % per, HEAD_SIZE)]

    def weight_block(j, origin):
        return wbuf.at[j // per, block_at(origin, deep), pl.ds(j % per * HEAD_SIZE, HEAD_SIZE)]

    def weight_local(j):
        return pltpu.make_async_copy(weight_source(j, core), weight_block(j, me), local.at[j])

    def weight_cross(j):
        return remote(
            weight_source(j, 1 - core), weight_block(j, me), w_cross.at[j], w_recv.at[j, me], {"ctx": partner}
        )

    def weight_copy(j, origin, way):
        block = weight_block(j, origin)
        return remote(
            block, block, w_send.at[j, origin, way], w_recv.at[j, origin], {"ctx": (me + 2, me - 2)[way]}
        )

    def weight_spread(j, origin):
        @pl.when(line < lines - 1)
        def _():
            weight_copy(j, origin, 0).start()

        @pl.when(line > 0)
        def _():
            weight_copy(j, origin, 1).start()

    def weight_own(j):
        weight_local(j).wait()
        weight_spread(j, me)
        weight_copy(j, partner, 0).wait_recv()
        weight_spread(j, partner)

    def weight_forward(j, hop):
        @pl.when((line >= hop) & (line < lines - 1))
        def _():
            for sub in range(2):
                origin = 2 * (line - hop) + sub
                weight_copy(j, origin, 0).wait_recv()
                weight_copy(j, origin, 0).start()

        @pl.when((line + hop < lines) & (line > 0))
        def _():
            for sub in range(2):
                origin = 2 * (line + hop) + sub
                weight_copy(j, origin, 1).wait_recv()
                weight_copy(j, origin, 1).start()

    def weight_join(j):
        @pl.when((line == 0) | (line == lines - 1))
        def _():
            @pl.loop(1, lines)
            def _(hop):
                for sub in range(2):
                    origin = 2 * jnp.where(line == 0, hop, lines - 1 - hop) + sub
                    weight_copy(j, origin, 0).wait_recv()


    def token_slice(index, m, part):
        columns = pl.ds(pl.multiple_of(index * slice_rows + part * part_rows, part_rows), part_rows)
        return tok.at[0, pl.ds(m * small, small), columns]

    def token_block(index, m, owner, part):
        return xbuf.at[index, m, owner, :, pl.ds(part * part_rows, part_rows)]

    def token_own(m):
        return tok.at[0, pl.ds(m * small, small), block_at(pipe, slice_rows)]

    def token_local(m):
        return pltpu.make_async_copy(token_own(m), xbuf.at[pipe, m, core], local.at[pieces + m])

    def token_cross(m, owner):
        return remote(token_own(m), xbuf.at[pipe, m, owner], xo_send.at[m], xo_recv.at[m], {"ctx": partner})

    def token_copy(d, m, part):
        to = lax.rem(pipe + d, pipes)
        return remote(
            token_slice(to, m, part), token_block(pipe, m, core, part),
            x_send.at[d - 1, m, part], x_recv.at[d - 1, m, part], {"pipe": to},
        )

    def token_relay(d, m, owner, part):
        block = token_block(lax.rem(pipe + pipes - d, pipes), m, owner, part)
        return remote(block, block, xr_send.at[d - 1, m, part], xr_recv.at[d - 1, m, part], {"ctx": partner})

    def token_arrived(d, m, part):
        block = token_block(lax.rem(pipe + pipes - d, pipes), m, core, part)
        to = lax.rem(pipe + d, pipes)
        remote(
            block, block, x_send.at[d - 1, m, part], x_recv.at[d - 1, m, part], {"pipe": to}
        ).wait_recv()


    def query_local():
        return pltpu.make_async_copy(
            qry.at[0, :, block_at(core, half_columns)], qbuf.at[block_at(core, rows)], local.at[pieces + 2]
        )

    def query_cross(place):
        return remote(
            qry.at[0, :, block_at(1 - core, half_columns)],
            qbuf.at[block_at(place, rows)], q_sem.at[0], q_sem.at[1], {"ctx": partner},
        )


    def rows_of(m):
        return pl.ds(0, 2) if m is None else pl.ds(m, 1)

    def partial_copy(j, m, d):
        to = lax.rem(pipe + d, pipes)
        return remote(
            pout.at[j, to, rows_of(m)], pin.at[j, d - 1, rows_of(m)],
            p_send.at[j, m or 0, d - 1], p_recv.at[j, m or 0, d - 1], {"pipe": to},
        )

    def multiply(which, first, stop, m):
        columns = slice(first * HEAD_SIZE, stop * HEAD_SIZE)
        count = 2 if m is None else 1
        place = slice(0, 2) if m is None else slice(m, m + 1)

        def product(index):
            left = xbuf[index, place].reshape(count * rows, slice_rows)
            return jnp.dot(left, wbuf[which, :, columns], preferred_element_type=jnp.float32)

        def part_of(value, h):
            value = value[:, (h - first) * HEAD_SIZE : (h - first + 1) * HEAD_SIZE]
            return value.reshape(count, rows, HEAD_SIZE)

        @pl.loop(1, pipes)
        def _(d):
            to = lax.rem(pipe + d, pipes)
            value = product(to)
            for h in range(first, stop):
                pout[which * per + h, to, place] = part_of(value, h).astype(pout.dtype)
            partial_copy(which * per + first, m, d).start()

        for h in range(first + 1, stop):
            for d in range(1, pipes):
                partial_copy(which * per + h, m, d).start()

        value = product(pipe)
        for h in range(first, stop):
            mine[which * per + h, place] = part_of(value, h)


    def kv_copy(j, m, origin, way):
        block = kvbuf.at[j, origin, rows_of(m)]
        return remote(
            block, block, kv_send.at[j, m or 0, origin, way], kv_recv.at[j, m or 0, origin],
            {"ctx": (me + 2, me - 2)[way]},
        )

    def total(j, m):
        place = slice(0, 2) if m is None else slice(m, m + 1)
        value = mine[j, place]
        for d in range(1, pipes):
            partial_copy(j, m, d).wait_recv()
            value = value + pin[j, d - 1, place].astype(jnp.float32)
        kvbuf[j, line, place] = value.astype(jnp.bfloat16)

        @pl.when(line < lines - 1)
        def _():
            kv_copy(j, m, line, 0).start()

        @pl.when(line > 0)
        def _():
            kv_copy(j, m, line, 1).start()

    def kv_forward(j, m, first, stop):
        @pl.loop(first, stop)
        def _(hop):
            @pl.when((line >= hop) & (line < lines - 1))
            def _():
                kv_copy(j, m, line - hop, 0).wait_recv()
                kv_copy(j, m, line - hop, 0).start()

            @pl.when((line + hop < lines) & (line > 0))
            def _():
                kv_copy(j, m, line + hop, 1).wait_recv()
                kv_copy(j, m, line + hop, 1).start()

    def kv_join(j, m):
        @pl.when((line == 0) | (line == lines - 1))
        def _():
            @pl.loop(1, lines)
            def _(hop):
                kv_copy(j, m, jnp.where(line == 0, hop, lines - 1 - hop), 0).wait_recv()


    factor = LOG2E / HEAD_SIZE**0.5
    outs = o_local.shape[0]
    out_columns = half_columns // outs
    middle = max(lines // 2, 2)

    def head_columns(head):
        return block_at(head, HEAD_SIZE)

    def soften(h, i):
        head = h * group + i
        score = lax.dot_general(
            qbuf[:, head_columns(head)], kvbuf[h].reshape(seq, HEAD_SIZE), (((1,), (1,)), ((), ())), preferred_element_type=jnp.float32
        )
        score = jnp.minimum(score, cap[...])
        largest = jnp.max(score, axis=1, keepdims=True)
        expo = jnp.exp2((score - largest) * factor)
        return expo.astype(jnp.bfloat16), jnp.sum(expo, axis=1, keepdims=True)

    def finish(h, i, weight, amount):
        summed = jnp.dot(weight, kvbuf[per + h].reshape(seq, HEAD_SIZE), preferred_element_type=jnp.float32)
        obuf[:, head_columns(h * group + i)] = (summed / amount).astype(jnp.bfloat16)

    def out_own(n):
        return pltpu.make_async_copy(
            obuf.at[block_at(core, rows), pl.ds(n * out_columns, out_columns)],
            out.at[0, :, block_at(core * outs + n, out_columns)],
            o_local.at[n],
        )

    def out_cross(n, owner):
        return remote(
            obuf.at[block_at(1 - core, rows), pl.ds(n * out_columns, out_columns)],
            out.at[0, :, block_at(owner * outs + n, out_columns)],
            o_send.at[n], o_recv.at[n], {"ctx": partner},
        )


    for j in range(pieces):
        weight_local(j).start()
    for m in range(2):
        token_local(m).start()
    query_local().start()

    barrier = pltpu.get_barrier_semaphore()
    for d in range(1, pipes):
        pl.semaphore_signal(barrier, inc=1, device_id={"pipe": lax.rem(pipe + d, pipes)}, device_id_type=MESH)
    pl.semaphore_signal(barrier, inc=1, device_id={"ctx": partner}, device_id_type=MESH)
    for step in range(1, lines):
        to = 2 * lax.rem(line + step, lines) + core
        pl.semaphore_signal(barrier, inc=1, device_id={"ctx": to}, device_id_type=MESH)
    pl.semaphore_wait(barrier, pipes + lines - 1)

    for j in range(pieces):
        weight_cross(j).start()
    weight_own(0)
    for m in range(2):
        for part in range(parts):
            for d in range(1, pipes):
                token_copy(d, m, part).start()
    weight_own(1)
    for m in range(2):
        token_cross(m, core).start()
    query_cross(core).start()

    lane = lax.broadcasted_iota(jnp.int32, (1, seq), 1)
    inside = lane % chip_rows
    lane = (lane // chip_rows) * chip_rows + inside % rows // small * rows + inside // rows * small + lane % small
    spot = jnp.zeros((1, seq), jnp.int32)
    for i in range(seq // half):
        spot = jnp.where(lane // half == i, order[i] * half, spot)
    key_position = spot + lane % half
    row = lax.broadcasted_iota(jnp.int32, (chip_rows, 1), 0)
    spot = jnp.zeros((chip_rows, 1), jnp.int32)
    per_line = chip_rows // half
    for i in range(per_line):
        spot = jnp.where(row // half == i, order[line * per_line + i] * half, spot)
    own_position = spot + row % half
    cap[...] = jnp.where(key_position <= own_position, jnp.inf, -jnp.inf)

    def tokens_ready(m):
        token_local(m).wait()
        for part in range(parts):
            for d in range(1, pipes):
                token_arrived(d, m, part)
                token_relay(d, m, core, part).start()
        token_cross(m, 1 - core).wait_recv()
        for part in range(parts):
            for d in range(1, pipes):
                token_relay(d, m, 1 - core, part).wait_recv()

    def weight_steps(first, stop):
        for step in range(first, stop):
            for hop in range(lines - 2, 0, -1):
                if 0 <= step - hop + 1 < pieces:
                    weight_forward(step - hop + 1, hop)
            if step + 2 < pieces:
                weight_own(step + 2)

    keys = range(per)
    last = pieces - 1
    weight_steps(0, per + lines - 3)
    tokens_ready(0)
    for j in keys:
        weight_join(j)
    multiply(0, 0, per, 0)
    weight_steps(per + lines - 3, pieces + lines - 3)
    tokens_ready(1)
    multiply(0, 0, per, 1)
    for j in range(per, last):
        weight_join(j)
        multiply(1, j - per, j - per + 1, None)

    @pl.when((line > 0) & (line < lines - 1))
    def _():
        multiply(1, per - 1, per, None)

    for j in keys:
        total(j, 0)
    for j in keys:
        kv_forward(j, 0, 1, middle)
    for j in keys:
        total(j, 1)
    for j in keys:
        kv_forward(j, 0, middle, lines - 1)

    @pl.when((line == 0) | (line == lines - 1))
    def _():
        weight_join(last)
        multiply(1, per - 1, per, None)

    for j in keys:
        kv_forward(j, 1, 1, middle)
    for j in range(per, last):
        total(j, None)
    for j in keys:
        kv_forward(j, 1, middle, lines - 1)
    total(last, None)

    def weights_drain():
        @pl.loop(0, lines)
        def _(other):
            for j in range(pieces):
                for sub in range(2):
                    origin = 2 * other + sub

                    @pl.when((other <= line) & (line < lines - 1))
                    def _():
                        weight_copy(j, origin, 0).wait_send()

                    @pl.when((other >= line) & (line > 0))
                    def _():
                        weight_copy(j, origin, 1).wait_send()

        for j in range(pieces):
            weight_cross(j).wait_send()

    def others_drain():
        query_cross(core).wait_send()
        for m in range(2):
            token_cross(m, core).wait_send()
        for d in range(1, pipes):
            for m in range(2):
                for part in range(parts):
                    token_copy(d, m, part).wait_send()
                    token_relay(d, m, core, part).wait_send()
                for j in keys:
                    partial_copy(j, m, d).wait_send()
            for j in range(per, pieces):
                partial_copy(j, None, d).wait_send()

    def soft_group(h, first, stop):
        @pl.loop(first, stop, unroll=2)
        def _(i):
            weight, amount = soften(h, i)
            pbuf[h * group + i] = weight
            abuf[h * group + i] = amount

    def finish_group(h, first, stop):
        @pl.loop(first, stop, unroll=4)
        def _(i):
            finish(h, i, pbuf[h * group + i], abuf[h * group + i])

    query_local().wait()
    query_cross(1 - core).wait_recv()
    some = group // 2
    for j in range(per, last):
        kv_forward(j, None, 1, middle)
    weights_drain()
    others_drain()
    for h in keys:
        kv_join(h, 0)
        kv_join(h, 1)
        soft_group(h, 0, some)
        if h == 0:
            for j in range(per, last):
                kv_forward(j, None, middle, lines - 1)
            kv_forward(last, None, 1, middle)
        if h == per - 1:
            kv_forward(last, None, middle, lines - 1)
        soft_group(h, some, group)
    for h in range(per):
        kv_join(per + h, None)
        for part in range(outs // per):
            finish_group(h, part * group * per // outs, (part + 1) * group * per // outs)
            out_own(h * outs // per + part).start()
            out_cross(h * outs // per + part, core).start()

    @pl.loop(0, lines)
    def _(other):
        for j, m in [(j, m) for j in keys for m in range(2)] + [(j, None) for j in range(per, pieces)]:

            @pl.when((other <= line) & (line < lines - 1))
            def _():
                kv_copy(j, m, other, 0).wait_send()

            @pl.when((other >= line) & (line > 0))
            def _():
                kv_copy(j, m, other, 1).wait_send()

    for n in range(outs):
        out_own(n).wait()
        out_cross(n, core).wait_send()
        out_cross(n, 1 - core).wait_recv()


def body(pipes, ctxs, tokens, queries, key_weight, value_weight, block_order):
    rows, width = tokens.shape[1:]
    deep, kv_width = key_weight.shape
    per = kv_width // HEAD_SIZE // 2
    pieces = 2 * per
    seq = rows * ctxs
    half = seq // block_order.shape[0]
    query_heads = queries.shape[2] // HEAD_SIZE // 2
    lines = ctxs // 2
    chip_rows = 2 * rows
    dma = pltpu.SemaphoreType.DMA
    any_space = pl.BlockSpec(memory_space=pl.ANY)
    return pl.pallas_call(
        functools.partial(kernel, pipes, ctxs, half),
        out_shape=jax.ShapeDtypeStruct(queries.shape, jnp.bfloat16),
        in_specs=[any_space] * 4 + [pl.BlockSpec(memory_space=pltpu.SMEM)],
        out_specs=any_space,
        scratch_shapes=[
            pltpu.VMEM((2, deep * ctxs, per * HEAD_SIZE), jnp.bfloat16),
            pltpu.VMEM((pipes, 2, 2, rows // 2, width // pipes), jnp.bfloat16),
            pltpu.VMEM((pieces, pipes, 2, rows, HEAD_SIZE), PARTIAL),
            pltpu.VMEM((pieces, pipes - 1, 2, rows, HEAD_SIZE), PARTIAL),
            pltpu.VMEM((pieces, 2, rows, HEAD_SIZE), jnp.float32),
            pltpu.VMEM((pieces, lines, 2, rows, HEAD_SIZE), jnp.bfloat16),
            pltpu.VMEM((chip_rows, queries.shape[2] // 2), jnp.bfloat16),
            pltpu.VMEM((chip_rows, seq), jnp.float32),
            pltpu.VMEM((query_heads, chip_rows, seq), jnp.bfloat16),
            pltpu.VMEM((query_heads, chip_rows, 1), jnp.float32),
            pltpu.VMEM((chip_rows, queries.shape[2] // 2), jnp.bfloat16),
            dma((pieces, ctxs, 2)),
            dma((pieces, ctxs)),
            dma((pieces,)),
            dma((pieces, 2, lines, 2)),
            dma((pieces, 2, lines)),
            dma((pipes - 1, 2, TOKEN_PARTS)),
            dma((pipes - 1, 2, TOKEN_PARTS)),
            dma((pipes - 1, 2, TOKEN_PARTS)),
            dma((pipes - 1, 2, TOKEN_PARTS)),
            dma((2,)),
            dma((2,)),
            dma((pieces, 2, pipes - 1)),
            dma((pieces, 2, pipes - 1)),
            dma((2,)),
            dma((2 * per,)),
            dma((2 * per,)),
            dma((2 * per,)),
            dma((pieces + 3,)),
        ],
        compiler_params=pltpu.CompilerParams(
            collective_id=0, has_side_effects=True, vmem_limit_bytes=VMEM_LIMIT
        ),
    )(tokens, queries, key_weight, value_weight, block_order)


def solution(mesh):
    return jax.shard_map(
        functools.partial(body, mesh.shape["pipe"], mesh.shape["ctx"]),
        mesh=mesh,
        in_specs=(
            P("pipe", "ctx", None),
            P("pipe", "ctx", None),
            P(("pipe", "ctx"), None),
            P(("pipe", "ctx"), None),
            P(),
        ),
        out_specs=P("pipe", "ctx", None),
        check_vma=False,
    )
```

```python
import functools

import jax
import jax.numpy as jnp
from jax import lax
from jax.experimental import pallas as pl
from jax.experimental.pallas import tpu as pltpu
from jax.sharding import PartitionSpec as P

HEAD_SIZE = 128
LOG2E = 1.4426950408889634
MESH = pl.DeviceIdType.MESH
PARTIAL = jnp.bfloat16
TOKEN_PARTS = 2
VMEM_LIMIT = 60 * 1024 * 1024


def block_at(index, size):
    return pl.ds(pl.multiple_of(index * size, size), size)


def remote(src, dst, send_sem, recv_sem, device_id):
    return pltpu.make_async_remote_copy(
        src_ref=src, dst_ref=dst, send_sem=send_sem, recv_sem=recv_sem, device_id=device_id, device_id_type=MESH
    )


def kernel(
    pipes, ctxs, half,
    tok, qry, kw, vw, order, out,
    wbuf, xbuf, pout, pin, mine, kvbuf, qbuf, cap, pbuf, abuf, obuf,
    w_send, w_recv, w_cross, kv_send, kv_recv, x_send, x_recv, xr_send, xr_recv, xo_send, xo_recv,
    p_send, p_recv, q_sem, o_send, o_recv, local,
):
    rows = 2 * xbuf.shape[3]
    small = xbuf.shape[3]
    slice_rows = xbuf.shape[4]
    parts = x_send.shape[2]
    part_rows = slice_rows // parts
    deep = kw.shape[0]
    lines = ctxs // 2
    heads = kw.shape[1] // HEAD_SIZE
    per = heads // 2
    pieces = 2 * per
    group = qbuf.shape[1] // (per * HEAD_SIZE)
    chip_rows = 2 * rows
    seq = ctxs * rows
    half_columns = qbuf.shape[1]
    pipe = lax.axis_index("pipe")
    me = lax.axis_index("ctx")
    line = me // 2
    core = me % 2
    partner = me + 1 - 2 * core


    def weight_source(j, to_core):
        return (kw, vw)[j // per].at[:, block_at(to_core * per + j % per, HEAD_SIZE)]

    def weight_block(j, origin):
        return wbuf.at[j // per, block_at(origin, deep), pl.ds(j % per * HEAD_SIZE, HEAD_SIZE)]

    def weight_local(j):
        return pltpu.make_async_copy(weight_source(j, core), weight_block(j, me), local.at[j])

    def weight_cross(j):
        return remote(
            weight_source(j, 1 - core), weight_block(j, me), w_cross.at[j], w_recv.at[j, me], {"ctx": partner}
        )

    def weight_copy(j, origin, way):
        block = weight_block(j, origin)
        return remote(
            block, block, w_send.at[j, origin, way], w_recv.at[j, origin], {"ctx": (me + 2, me - 2)[way]}
        )

    def weight_spread(j, origin):
        @pl.when(line < lines - 1)
        def _():
            weight_copy(j, origin, 0).start()

        @pl.when(line > 0)
        def _():
            weight_copy(j, origin, 1).start()

    def weight_own(j):
        weight_local(j).wait()
        weight_spread(j, me)
        weight_copy(j, partner, 0).wait_recv()
        weight_spread(j, partner)

    def weight_forward(j, hop):
        @pl.when((line >= hop) & (line < lines - 1))
        def _():
            for sub in range(2):
                origin = 2 * (line - hop) + sub
                weight_copy(j, origin, 0).wait_recv()
                weight_copy(j, origin, 0).start()

        @pl.when((line + hop < lines) & (line > 0))
        def _():
            for sub in range(2):
                origin = 2 * (line + hop) + sub
                weight_copy(j, origin, 1).wait_recv()
                weight_copy(j, origin, 1).start()

    def weight_join(j):
        @pl.when((line == 0) | (line == lines - 1))
        def _():
            @pl.loop(1, lines)
            def _(hop):
                for sub in range(2):
                    origin = 2 * jnp.where(line == 0, hop, lines - 1 - hop) + sub
                    weight_copy(j, origin, 0).wait_recv()


    def token_slice(index, m, part):
        columns = pl.ds(pl.multiple_of(index * slice_rows + part * part_rows, part_rows), part_rows)
        return tok.at[0, pl.ds(m * small, small), columns]

    def token_block(index, m, owner, part):
        return xbuf.at[index, m, owner, :, pl.ds(part * part_rows, part_rows)]

    def token_own(m):
        return tok.at[0, pl.ds(m * small, small), block_at(pipe, slice_rows)]

    def token_local(m):
        return pltpu.make_async_copy(token_own(m), xbuf.at[pipe, m, core], local.at[pieces + m])

    def token_cross(m, owner):
        return remote(token_own(m), xbuf.at[pipe, m, owner], xo_send.at[m], xo_recv.at[m], {"ctx": partner})

    def token_copy(d, m, part):
        to = lax.rem(pipe + d, pipes)
        return remote(
            token_slice(to, m, part), token_block(pipe, m, core, part),
            x_send.at[d - 1, m, part], x_recv.at[d - 1, m, part], {"pipe": to},
        )

    def token_relay(d, m, owner, part):
        block = token_block(lax.rem(pipe + pipes - d, pipes), m, owner, part)
        return remote(block, block, xr_send.at[d - 1, m, part], xr_recv.at[d - 1, m, part], {"ctx": partner})

    def token_arrived(d, m, part):
        block = token_block(lax.rem(pipe + pipes - d, pipes), m, core, part)
        to = lax.rem(pipe + d, pipes)
        remote(
            block, block, x_send.at[d - 1, m, part], x_recv.at[d - 1, m, part], {"pipe": to}
        ).wait_recv()


    def query_local():
        return pltpu.make_async_copy(
            qry.at[0, :, block_at(core, half_columns)], qbuf.at[pl.ds(0, rows)], local.at[pieces + 2]
        )

    def query_cross():
        return remote(
            qry.at[0, :, block_at(1 - core, half_columns)],
            qbuf.at[pl.ds(rows, rows)], q_sem.at[0], q_sem.at[1], {"ctx": partner},
        )


    def rows_of(m):
        return pl.ds(0, 2) if m is None else pl.ds(m, 1)

    def partial_copy(j, m, d):
        to = lax.rem(pipe + d, pipes)
        return remote(
            pout.at[j, to, rows_of(m)], pin.at[j, d - 1, rows_of(m)],
            p_send.at[j, m or 0, d - 1], p_recv.at[j, m or 0, d - 1], {"pipe": to},
        )

    def multiply(which, first, stop, m):
        columns = slice(first * HEAD_SIZE, stop * HEAD_SIZE)
        count = 2 if m is None else 1
        place = slice(0, 2) if m is None else slice(m, m + 1)

        def product(index):
            left = xbuf[index, place].reshape(count * rows, slice_rows)
            return jnp.dot(left, wbuf[which, :, columns], preferred_element_type=jnp.float32)

        def part_of(value, h):
            value = value[:, (h - first) * HEAD_SIZE : (h - first + 1) * HEAD_SIZE]
            return value.reshape(count, rows, HEAD_SIZE)

        @pl.loop(1, pipes)
        def _(d):
            to = lax.rem(pipe + d, pipes)
            value = product(to)
            for h in range(first, stop):
                pout[which * per + h, to, place] = part_of(value, h).astype(pout.dtype)
            partial_copy(which * per + first, m, d).start()

        for h in range(first + 1, stop):
            for d in range(1, pipes):
                partial_copy(which * per + h, m, d).start()

        value = product(pipe)
        for h in range(first, stop):
            mine[which * per + h, place] = part_of(value, h)


    def kv_copy(j, m, origin, way):
        block = kvbuf.at[j, origin, rows_of(m)]
        return remote(
            block, block, kv_send.at[j, m or 0, origin, way], kv_recv.at[j, m or 0, origin],
            {"ctx": (me + 2, me - 2)[way]},
        )

    def total(j, m):
        place = slice(0, 2) if m is None else slice(m, m + 1)
        value = mine[j, place]
        for d in range(1, pipes):
            partial_copy(j, m, d).wait_recv()
            value = value + pin[j, d - 1, place].astype(jnp.float32)
        kvbuf[j, line, place] = value.astype(jnp.bfloat16)

        @pl.when(line < lines - 1)
        def _():
            kv_copy(j, m, line, 0).start()

        @pl.when(line > 0)
        def _():
            kv_copy(j, m, line, 1).start()

    def kv_forward(j, m, first, stop):
        @pl.loop(first, stop)
        def _(hop):
            @pl.when((line >= hop) & (line < lines - 1))
            def _():
                kv_copy(j, m, line - hop, 0).wait_recv()
                kv_copy(j, m, line - hop, 0).start()

            @pl.when((line + hop < lines) & (line > 0))
            def _():
                kv_copy(j, m, line + hop, 1).wait_recv()
                kv_copy(j, m, line + hop, 1).start()

    def kv_join(j, m):
        @pl.when((line == 0) | (line == lines - 1))
        def _():
            @pl.loop(1, lines)
            def _(hop):
                kv_copy(j, m, jnp.where(line == 0, hop, lines - 1 - hop), 0).wait_recv()


    factor = LOG2E / HEAD_SIZE**0.5
    outs = o_send.shape[0]
    out_columns = half_columns // outs
    middle = max(lines // 2, 2)

    def head_columns(head):
        return block_at(head, HEAD_SIZE)

    def soften(h, i):
        head = h * group + i
        score = lax.dot_general(
            qbuf[:, head_columns(head)], kvbuf[h].reshape(seq, HEAD_SIZE), (((1,), (1,)), ((), ())), preferred_element_type=jnp.float32
        )
        score = jnp.minimum(score, cap[...])
        largest = jnp.max(score, axis=1, keepdims=True)
        expo = jnp.exp2((score - largest) * factor)
        return expo.astype(jnp.bfloat16), jnp.sum(expo, axis=1, keepdims=True)

    def finish(h, i, weight, amount):
        summed = jnp.dot(weight, kvbuf[per + h].reshape(seq, HEAD_SIZE), preferred_element_type=jnp.float32)
        value = (summed / amount).astype(jnp.bfloat16)
        out[0, :, head_columns(core * per * group + h * group + i)] = value[:rows]
        obuf[:, head_columns(h * group + i)] = value[rows:]

    def out_cross(n, owner):
        return remote(
            obuf.at[:, pl.ds(n * out_columns, out_columns)],
            out.at[0, :, block_at(owner * outs + n, out_columns)],
            o_send.at[n], o_recv.at[n], {"ctx": partner},
        )


    for j in range(pieces):
        weight_local(j).start()
    for m in range(2):
        token_local(m).start()
    query_local().start()

    barrier = pltpu.get_barrier_semaphore()
    for d in range(1, pipes):
        pl.semaphore_signal(barrier, inc=1, device_id={"pipe": lax.rem(pipe + d, pipes)}, device_id_type=MESH)
    pl.semaphore_signal(barrier, inc=1, device_id={"ctx": partner}, device_id_type=MESH)
    for step in range(1, lines):
        to = 2 * lax.rem(line + step, lines) + core
        pl.semaphore_signal(barrier, inc=1, device_id={"ctx": to}, device_id_type=MESH)
    pl.semaphore_wait(barrier, pipes + lines - 1)

    for j in range(pieces):
        weight_cross(j).start()
    weight_own(0)
    for m in range(2):
        for part in range(parts):
            for d in range(1, pipes):
                token_copy(d, m, part).start()
    weight_own(1)
    for m in range(2):
        token_cross(m, core).start()
    query_cross().start()

    lane = lax.broadcasted_iota(jnp.int32, (1, seq), 1)
    inside = lane % chip_rows
    lane = (lane // chip_rows) * chip_rows + inside % rows // small * rows + inside // rows * small + lane % small
    spot = jnp.zeros((1, seq), jnp.int32)
    for i in range(seq // half):
        spot = jnp.where(lane // half == i, order[i] * half, spot)
    key_position = spot + lane % half
    row = lax.broadcasted_iota(jnp.int32, (chip_rows, 1), 0)
    row = jnp.where(row < rows, row + core * rows, row - core * rows)
    spot = jnp.zeros((chip_rows, 1), jnp.int32)
    per_line = chip_rows // half
    for i in range(per_line):
        spot = jnp.where(row // half == i, order[line * per_line + i] * half, spot)
    own_position = spot + row % half
    cap[...] = jnp.where(key_position <= own_position, jnp.inf, -jnp.inf)

    def tokens_ready(m):
        token_local(m).wait()
        for part in range(parts):
            for d in range(1, pipes):
                token_arrived(d, m, part)
                token_relay(d, m, core, part).start()
        token_cross(m, 1 - core).wait_recv()
        for part in range(parts):
            for d in range(1, pipes):
                token_relay(d, m, 1 - core, part).wait_recv()

    def weight_steps(first, stop):
        for step in range(first, stop):
            for hop in range(lines - 2, 0, -1):
                if 0 <= step - hop + 1 < pieces:
                    weight_forward(step - hop + 1, hop)
            if step + 2 < pieces:
                weight_own(step + 2)

    keys = range(per)
    last = pieces - 1
    weight_steps(0, per + lines - 3)
    tokens_ready(0)
    for j in keys:
        weight_join(j)
    multiply(0, 0, per, 0)
    weight_steps(per + lines - 3, pieces + lines - 3)
    tokens_ready(1)
    multiply(0, 0, per, 1)
    for j in range(per, last):
        weight_join(j)
        multiply(1, j - per, j - per + 1, None)

    @pl.when((line > 0) & (line < lines - 1))
    def _():
        multiply(1, per - 1, per, None)

    for j in keys:
        total(j, 0)
    for j in keys:
        kv_forward(j, 0, 1, middle)
    for j in keys:
        total(j, 1)
    for j in keys:
        kv_forward(j, 0, middle, lines - 1)

    @pl.when((line == 0) | (line == lines - 1))
    def _():
        weight_join(last)
        multiply(1, per - 1, per, None)

    for j in keys:
        kv_forward(j, 1, 1, middle)
    for j in range(per, last):
        total(j, None)
    for j in keys:
        kv_forward(j, 1, middle, lines - 1)
    total(last, None)

    def weights_drain():
        @pl.loop(0, lines)
        def _(other):
            for j in range(pieces):
                for sub in range(2):
                    origin = 2 * other + sub

                    @pl.when((other <= line) & (line < lines - 1))
                    def _():
                        weight_copy(j, origin, 0).wait_send()

                    @pl.when((other >= line) & (line > 0))
                    def _():
                        weight_copy(j, origin, 1).wait_send()

        for j in range(pieces):
            weight_cross(j).wait_send()

    def others_drain():
        query_cross().wait_send()
        for m in range(2):
            token_cross(m, core).wait_send()
        for d in range(1, pipes):
            for m in range(2):
                for part in range(parts):
                    token_copy(d, m, part).wait_send()
                    token_relay(d, m, core, part).wait_send()
                for j in keys:
                    partial_copy(j, m, d).wait_send()
            for j in range(per, pieces):
                partial_copy(j, None, d).wait_send()

    def soft_group(h, first, stop):
        @pl.loop(first, stop, unroll=2)
        def _(i):
            weight, amount = soften(h, i)
            pbuf[h * group + i] = weight
            abuf[h * group + i] = amount

    def finish_group(h, first, stop):
        @pl.loop(first, stop, unroll=4)
        def _(i):
            finish(h, i, pbuf[h * group + i], abuf[h * group + i])

    query_local().wait()
    query_cross().wait_recv()
    some = group // 2
    for j in range(per, last):
        kv_forward(j, None, 1, middle)
    weights_drain()
    others_drain()
    for h in keys:
        kv_join(h, 0)
        kv_join(h, 1)
        soft_group(h, 0, some)
        if h == 0:
            for j in range(per, last):
                kv_forward(j, None, middle, lines - 1)
            kv_forward(last, None, 1, middle)
        if h == per - 1:
            kv_forward(last, None, middle, lines - 1)
        soft_group(h, some, group)
    def kv_drain(units):
        @pl.loop(0, lines)
        def _(other):
            for j, m in units:

                @pl.when((other <= line) & (line < lines - 1))
                def _():
                    kv_copy(j, m, other, 0).wait_send()

                @pl.when((other >= line) & (line > 0))
                def _():
                    kv_copy(j, m, other, 1).wait_send()

    for h in range(per):
        kv_join(per + h, None)
        for part in range(outs // per):
            finish_group(h, part * group * per // outs, (part + 1) * group * per // outs)
            out_cross(h * outs // per + part, core).start()
        if h == 0:
            kv_drain([(j, m) for j in keys for m in range(2)] + [(j, None) for j in range(per, last)])
    kv_drain([(last, None)])
    for n in range(outs):
        out_cross(n, core).wait_send()
        out_cross(n, 1 - core).wait_recv()


def body(pipes, ctxs, tokens, queries, key_weight, value_weight, block_order):
    rows, width = tokens.shape[1:]
    deep, kv_width = key_weight.shape
    per = kv_width // HEAD_SIZE // 2
    pieces = 2 * per
    seq = rows * ctxs
    half = seq // block_order.shape[0]
    query_heads = queries.shape[2] // HEAD_SIZE // 2
    lines = ctxs // 2
    chip_rows = 2 * rows
    dma = pltpu.SemaphoreType.DMA
    any_space = pl.BlockSpec(memory_space=pl.ANY)
    return pl.pallas_call(
        functools.partial(kernel, pipes, ctxs, half),
        out_shape=pltpu.VMEM(queries.shape, jnp.bfloat16),
        in_specs=[any_space] * 4 + [pl.BlockSpec(memory_space=pltpu.SMEM)],
        out_specs=pl.BlockSpec(memory_space=pltpu.VMEM),
        scratch_shapes=[
            pltpu.VMEM((2, deep * ctxs, per * HEAD_SIZE), jnp.bfloat16),
            pltpu.VMEM((pipes, 2, 2, rows // 2, width // pipes), jnp.bfloat16),
            pltpu.VMEM((pieces, pipes, 2, rows, HEAD_SIZE), PARTIAL),
            pltpu.VMEM((pieces, pipes - 1, 2, rows, HEAD_SIZE), PARTIAL),
            pltpu.VMEM((pieces, 2, rows, HEAD_SIZE), jnp.float32),
            pltpu.VMEM((pieces, lines, 2, rows, HEAD_SIZE), jnp.bfloat16),
            pltpu.VMEM((chip_rows, queries.shape[2] // 2), jnp.bfloat16),
            pltpu.VMEM((chip_rows, seq), jnp.float32),
            pltpu.VMEM((query_heads, chip_rows, seq), jnp.bfloat16),
            pltpu.VMEM((query_heads, chip_rows, 1), jnp.float32),
            pltpu.VMEM((rows, queries.shape[2] // 2), jnp.bfloat16),
            dma((pieces, ctxs, 2)),
            dma((pieces, ctxs)),
            dma((pieces,)),
            dma((pieces, 2, lines, 2)),
            dma((pieces, 2, lines)),
            dma((pipes - 1, 2, TOKEN_PARTS)),
            dma((pipes - 1, 2, TOKEN_PARTS)),
            dma((pipes - 1, 2, TOKEN_PARTS)),
            dma((pipes - 1, 2, TOKEN_PARTS)),
            dma((2,)),
            dma((2,)),
            dma((pieces, 2, pipes - 1)),
            dma((pieces, 2, pipes - 1)),
            dma((2,)),
            dma((2 * per,)),
            dma((2 * per,)),
            dma((pieces + 3,)),
        ],
        compiler_params=pltpu.CompilerParams(
            collective_id=0, has_side_effects=True, vmem_limit_bytes=VMEM_LIMIT
        ),
    )(tokens, queries, key_weight, value_weight, block_order)


def solution(mesh):
    return jax.shard_map(
        functools.partial(body, mesh.shape["pipe"], mesh.shape["ctx"]),
        mesh=mesh,
        in_specs=(
            P("pipe", "ctx", None),
            P("pipe", "ctx", None),
            P(("pipe", "ctx"), None),
            P(("pipe", "ctx"), None),
            P(),
        ),
        out_specs=P("pipe", "ctx", None),
        check_vma=False,
    )
```

```python
import functools

import jax
import jax.numpy as jnp
from jax import lax
from jax.experimental import pallas as pl
from jax.experimental.pallas import tpu as pltpu
from jax.sharding import PartitionSpec as P

HEAD_SIZE = 128
LOG2E = 1.4426950408889634
MESH = pl.DeviceIdType.MESH
PARTIAL = jnp.bfloat16
TOKEN_PARTS = 2
VMEM_LIMIT = 60 * 1024 * 1024


def block_at(index, size):
    return pl.ds(pl.multiple_of(index * size, size), size)


def remote(src, dst, send_sem, recv_sem, device_id):
    return pltpu.make_async_remote_copy(
        src_ref=src, dst_ref=dst, send_sem=send_sem, recv_sem=recv_sem, device_id=device_id, device_id_type=MESH
    )


def kernel(
    pipes, ctxs, half,
    tok, qry, kw, vw, order, out,
    wbuf, xbuf, pout, pin, mine, kvbuf, qbuf, cap, pbuf, abuf, obuf,
    w_send, w_recv, w_cross, kv_send, kv_recv, x_send, x_recv, xr_send, xr_recv, xo_send, xo_recv,
    p_send, p_recv, q_sem, o_send, o_recv, local,
):
    rows = 2 * xbuf.shape[3]
    small = xbuf.shape[3]
    slice_rows = xbuf.shape[4]
    parts = x_send.shape[2]
    part_rows = slice_rows // parts
    deep = kw.shape[0]
    lines = ctxs // 2
    heads = kw.shape[1] // HEAD_SIZE
    per = heads // 2
    pieces = 2 * per
    group = qbuf.shape[1] // (per * HEAD_SIZE)
    chip_rows = 2 * rows
    seq = ctxs * rows
    half_columns = qbuf.shape[1]
    pipe = lax.axis_index("pipe")
    me = lax.axis_index("ctx")
    line = me // 2
    core = me % 2
    partner = me + 1 - 2 * core


    def weight_source(j, to_core):
        return (kw, vw)[j // per].at[:, block_at(to_core * per + j % per, HEAD_SIZE)]

    def weight_block(j, origin):
        return wbuf.at[j // per, block_at(origin, deep), pl.ds(j % per * HEAD_SIZE, HEAD_SIZE)]

    def weight_local(j):
        return pltpu.make_async_copy(weight_source(j, core), weight_block(j, me), local.at[j])

    def weight_cross(j):
        return remote(
            weight_source(j, 1 - core), weight_block(j, me), w_cross.at[j], w_recv.at[j, me], {"ctx": partner}
        )

    def weight_copy(j, origin, way):
        block = weight_block(j, origin)
        return remote(
            block, block, w_send.at[j, origin, way], w_recv.at[j, origin], {"ctx": (me + 2, me - 2)[way]}
        )

    def weight_spread(j, origin):
        @pl.when(line < lines - 1)
        def _():
            weight_copy(j, origin, 0).start()

        @pl.when(line > 0)
        def _():
            weight_copy(j, origin, 1).start()

    def weight_own(j):
        weight_local(j).wait()
        weight_spread(j, me)
        weight_copy(j, partner, 0).wait_recv()
        weight_spread(j, partner)

    def weight_forward(j, hop):
        @pl.when((line >= hop) & (line < lines - 1))
        def _():
            for sub in range(2):
                origin = 2 * (line - hop) + sub
                weight_copy(j, origin, 0).wait_recv()
                weight_copy(j, origin, 0).start()

        @pl.when((line + hop < lines) & (line > 0))
        def _():
            for sub in range(2):
                origin = 2 * (line + hop) + sub
                weight_copy(j, origin, 1).wait_recv()
                weight_copy(j, origin, 1).start()

    def weight_join(j):
        @pl.when((line == 0) | (line == lines - 1))
        def _():
            @pl.loop(1, lines)
            def _(hop):
                for sub in range(2):
                    origin = 2 * jnp.where(line == 0, hop, lines - 1 - hop) + sub
                    weight_copy(j, origin, 0).wait_recv()


    def token_slice(index, m, part):
        columns = pl.ds(pl.multiple_of(index * slice_rows + part * part_rows, part_rows), part_rows)
        return tok.at[0, pl.ds(m * small, small), columns]

    def token_block(index, m, owner, part):
        return xbuf.at[index, m, owner, :, pl.ds(part * part_rows, part_rows)]

    def token_own(m):
        return tok.at[0, pl.ds(m * small, small), block_at(pipe, slice_rows)]

    def token_local(m):
        return pltpu.make_async_copy(token_own(m), xbuf.at[pipe, m, core], local.at[pieces + m])

    def token_cross(m, owner):
        return remote(token_own(m), xbuf.at[pipe, m, owner], xo_send.at[m], xo_recv.at[m], {"ctx": partner})

    def token_copy(d, m, part):
        to = lax.rem(pipe + d, pipes)
        return remote(
            token_slice(to, m, part), token_block(pipe, m, core, part),
            x_send.at[d - 1, m, part], x_recv.at[d - 1, m, part], {"pipe": to},
        )

    def token_relay(d, m, owner, part):
        block = token_block(lax.rem(pipe + pipes - d, pipes), m, owner, part)
        return remote(block, block, xr_send.at[d - 1, m, part], xr_recv.at[d - 1, m, part], {"ctx": partner})

    def token_arrived(d, m, part):
        block = token_block(lax.rem(pipe + pipes - d, pipes), m, core, part)
        to = lax.rem(pipe + d, pipes)
        remote(
            block, block, x_send.at[d - 1, m, part], x_recv.at[d - 1, m, part], {"pipe": to}
        ).wait_recv()


    def query_local():
        return pltpu.make_async_copy(
            qry.at[0, :, block_at(core, half_columns)], qbuf.at[pl.ds(0, rows)], local.at[pieces + 2]
        )

    def query_cross():
        return remote(
            qry.at[0, :, block_at(1 - core, half_columns)],
            qbuf.at[pl.ds(rows, rows)], q_sem.at[0], q_sem.at[1], {"ctx": partner},
        )


    def rows_of(m):
        return pl.ds(0, 2) if m is None else pl.ds(m, 1)

    def partial_copy(j, m, d):
        to = lax.rem(pipe + d, pipes)
        return remote(
            pout.at[j, to, rows_of(m)], pin.at[j, d - 1, rows_of(m)],
            p_send.at[j, m or 0, d - 1], p_recv.at[j, m or 0, d - 1], {"pipe": to},
        )

    def multiply(which, first, stop, m):
        columns = slice(first * HEAD_SIZE, stop * HEAD_SIZE)
        count = 2 if m is None else 1
        place = slice(0, 2) if m is None else slice(m, m + 1)

        def product(index):
            left = xbuf[index, place].reshape(count * rows, slice_rows)
            return jnp.dot(left, wbuf[which, :, columns], preferred_element_type=jnp.float32)

        def part_of(value, h):
            value = value[:, (h - first) * HEAD_SIZE : (h - first + 1) * HEAD_SIZE]
            return value.reshape(count, rows, HEAD_SIZE)

        @pl.loop(1, pipes)
        def _(d):
            to = lax.rem(pipe + d, pipes)
            value = product(to)
            for h in range(first, stop):
                pout[which * per + h, to, place] = part_of(value, h).astype(pout.dtype)
            partial_copy(which * per + first, m, d).start()

        for h in range(first + 1, stop):
            for d in range(1, pipes):
                partial_copy(which * per + h, m, d).start()

        value = product(pipe)
        for h in range(first, stop):
            mine[which * per + h, place] = part_of(value, h)


    def kv_copy(j, m, origin, way):
        block = kvbuf.at[j, origin, rows_of(m)]
        return remote(
            block, block, kv_send.at[j, m or 0, origin, way], kv_recv.at[j, m or 0, origin],
            {"ctx": (me + 2, me - 2)[way]},
        )

    def total(j, m):
        place = slice(0, 2) if m is None else slice(m, m + 1)
        value = mine[j, place]
        for d in range(1, pipes):
            partial_copy(j, m, d).wait_recv()
            value = value + pin[j, d - 1, place].astype(jnp.float32)
        kvbuf[j, line, place] = value.astype(jnp.bfloat16)

        @pl.when(line < lines - 1)
        def _():
            kv_copy(j, m, line, 0).start()

        @pl.when(line > 0)
        def _():
            kv_copy(j, m, line, 1).start()

    def kv_forward(j, m, first, stop):
        @pl.loop(first, stop)
        def _(hop):
            @pl.when((line >= hop) & (line < lines - 1))
            def _():
                kv_copy(j, m, line - hop, 0).wait_recv()
                kv_copy(j, m, line - hop, 0).start()

            @pl.when((line + hop < lines) & (line > 0))
            def _():
                kv_copy(j, m, line + hop, 1).wait_recv()
                kv_copy(j, m, line + hop, 1).start()

    def kv_join(j, m, first=1, stop=None):
        @pl.when((line == 0) | (line == lines - 1))
        def _():
            @pl.loop(first, lines if stop is None else stop)
            def _(hop):
                kv_copy(j, m, jnp.where(line == 0, hop, lines - 1 - hop), 0).wait_recv()


    factor = LOG2E / HEAD_SIZE**0.5
    outs = o_send.shape[0]
    out_columns = half_columns // outs
    middle = max(lines // 2, 2)

    def head_columns(head):
        return block_at(head, HEAD_SIZE)

    def soften(h, i):
        head = h * group + i
        score = lax.dot_general(
            qbuf[:, head_columns(head)], kvbuf[h].reshape(seq, HEAD_SIZE), (((1,), (1,)), ((), ())), preferred_element_type=jnp.float32
        )
        score = jnp.minimum(score, cap[...])
        largest = jnp.max(score, axis=1, keepdims=True)
        expo = jnp.exp2((score - largest) * factor)
        return expo.astype(jnp.bfloat16), jnp.sum(expo, axis=1, keepdims=True)

    def values_of(h, first, count):
        return kvbuf[per + h, pl.ds(first, count)].reshape(count * chip_rows, HEAD_SIZE)

    def own_out(h, i):
        return out.at[0, :, head_columns(core * per * group + h * group + i)]

    def finish(h, i):
        head = h * group + i
        summed = jnp.dot(pbuf[head], values_of(h, 0, lines), preferred_element_type=jnp.float32)
        value = (summed / abuf[head]).astype(jnp.bfloat16)
        own_out(h, i)[...] = value[:rows]
        obuf[:, head_columns(head)] = value[rows:]


    def finish_far(h, i, place):
        summed = jnp.dot(pbuf[h * group + i, place], values_of(h, 0, lines), preferred_element_type=jnp.float32)
        return (summed / abuf[h * group + i, place]).astype(jnp.bfloat16)

    def out_cross(n, owner):
        return remote(
            obuf.at[:, pl.ds(n * out_columns, out_columns)],
            out.at[0, :, block_at(owner * outs + n, out_columns)],
            o_send.at[n], o_recv.at[n], {"ctx": partner},
        )


    for j in range(pieces):
        weight_local(j).start()
    for m in range(2):
        token_local(m).start()
    query_local().start()

    barrier = pltpu.get_barrier_semaphore()
    for d in range(1, pipes):
        pl.semaphore_signal(barrier, inc=1, device_id={"pipe": lax.rem(pipe + d, pipes)}, device_id_type=MESH)
    pl.semaphore_signal(barrier, inc=1, device_id={"ctx": partner}, device_id_type=MESH)
    for step in range(1, lines):
        to = 2 * lax.rem(line + step, lines) + core
        pl.semaphore_signal(barrier, inc=1, device_id={"ctx": to}, device_id_type=MESH)
    pl.semaphore_wait(barrier, pipes + lines - 1)

    for j in range(pieces):
        weight_cross(j).start()
    weight_own(0)
    for m in range(2):
        for part in range(parts):
            for d in range(1, pipes):
                token_copy(d, m, part).start()
    weight_own(1)
    for m in range(2):
        token_cross(m, core).start()
    query_cross().start()

    lane = lax.broadcasted_iota(jnp.int32, (1, seq), 1)
    inside = lane % chip_rows
    lane = (lane // chip_rows) * chip_rows + inside % rows // small * rows + inside // rows * small + lane % small
    spot = jnp.zeros((1, seq), jnp.int32)
    for i in range(seq // half):
        spot = jnp.where(lane // half == i, order[i] * half, spot)
    key_position = spot + lane % half
    row = lax.broadcasted_iota(jnp.int32, (chip_rows, 1), 0)
    row = jnp.where(row < rows, row + core * rows, row - core * rows)
    spot = jnp.zeros((chip_rows, 1), jnp.int32)
    per_line = chip_rows // half
    for i in range(per_line):
        spot = jnp.where(row // half == i, order[line * per_line + i] * half, spot)
    own_position = spot + row % half
    cap[...] = jnp.where(key_position <= own_position, jnp.inf, -jnp.inf)

    def tokens_ready(m):
        token_local(m).wait()
        for part in range(parts):
            for d in range(1, pipes):
                token_arrived(d, m, part)
                token_relay(d, m, core, part).start()
        token_cross(m, 1 - core).wait_recv()
        for part in range(parts):
            for d in range(1, pipes):
                token_relay(d, m, 1 - core, part).wait_recv()

    def weight_steps(first, stop):
        for step in range(first, stop):
            for hop in range(lines - 2, 0, -1):
                if 0 <= step - hop + 1 < pieces:
                    weight_forward(step - hop + 1, hop)
            if step + 2 < pieces:
                weight_own(step + 2)

    keys = range(per)
    last = pieces - 1
    weight_steps(0, per + lines - 3)
    tokens_ready(0)
    for j in keys:
        weight_join(j)
    multiply(0, 0, per, 0)
    weight_steps(per + lines - 3, pieces + lines - 3)
    tokens_ready(1)
    multiply(0, 0, per, 1)
    for j in keys:
        total(j, 0)
    for j in range(per, last):
        weight_join(j)
        multiply(1, j - per, j - per + 1, None)

    @pl.when((line > 0) & (line < lines - 1))
    def _():
        multiply(1, per - 1, per, None)

    for j in keys:
        kv_forward(j, 0, 1, middle)
    for j in keys:
        total(j, 1)
    for j in keys:
        kv_forward(j, 0, middle, lines - 1)

    @pl.when((line == 0) | (line == lines - 1))
    def _():
        weight_join(last)
        multiply(1, per - 1, per, None)

    for j in keys:
        kv_forward(j, 1, 1, middle)
    for j in range(per, last):
        total(j, None)
    for j in keys:
        kv_forward(j, 1, middle, lines - 1)
    total(last, None)

    def weights_drain():
        @pl.loop(0, lines)
        def _(other):
            for j in range(pieces):
                for sub in range(2):
                    origin = 2 * other + sub

                    @pl.when((other <= line) & (line < lines - 1))
                    def _():
                        weight_copy(j, origin, 0).wait_send()

                    @pl.when((other >= line) & (line > 0))
                    def _():
                        weight_copy(j, origin, 1).wait_send()

        for j in range(pieces):
            weight_cross(j).wait_send()

    def others_drain():
        query_cross().wait_send()
        for m in range(2):
            token_cross(m, core).wait_send()
        for d in range(1, pipes):
            for m in range(2):
                for part in range(parts):
                    token_copy(d, m, part).wait_send()
                    token_relay(d, m, core, part).wait_send()
                for j in keys:
                    partial_copy(j, m, d).wait_send()
            for j in range(per, pieces):
                partial_copy(j, None, d).wait_send()

    def soft_group(h, first, stop):
        @pl.loop(first, stop, unroll=2)
        def _(i):
            weight, amount = soften(h, i)
            pbuf[h * group + i] = weight
            abuf[h * group + i] = amount

    def finish_group(h, first, stop):
        @pl.loop(first, stop, unroll=4)
        def _(i):
            finish(h, i)

    query_local().wait()
    query_cross().wait_recv()
    some = group // 2
    for j in range(per, last):
        kv_forward(j, None, 1, middle)
    weights_drain()
    others_drain()
    for h in keys:
        kv_join(h, 0)
        kv_join(h, 1)
        soft_group(h, 0, some)
        if h == 0:
            for j in range(per, last):
                kv_forward(j, None, middle, lines - 1)
            kv_forward(last, None, 1, middle)
        if h == per - 1:
            kv_forward(last, None, middle, lines - 1)
        soft_group(h, some, group)
    def kv_drain(units):
        @pl.loop(0, lines)
        def _(other):
            for j, m in units:

                @pl.when((other <= line) & (line < lines - 1))
                def _():
                    kv_copy(j, m, other, 0).wait_send()

                @pl.when((other >= line) & (line > 0))
                def _():
                    kv_copy(j, m, other, 1).wait_send()

    for h in range(per - 1):
        kv_join(per + h, None)
        for part in range(outs // per):
            finish_group(h, part * group * per // outs, (part + 1) * group * per // outs)
            out_cross(h * outs // per + part, core).start()
    kv_drain([(j, m) for j in keys for m in range(2)] + [(j, None) for j in range(per, last)])
    kv_join(last, None)

    @pl.loop(0, group, unroll=4)
    def _(i):
        obuf[:, head_columns((per - 1) * group + i)] = finish_far(per - 1, i, slice(rows, chip_rows))

    for n in range(outs - outs // per, outs):
        out_cross(n, core).start()

    @pl.loop(0, group, unroll=4)
    def _(i):
        own_out(per - 1, i)[...] = finish_far(per - 1, i, slice(0, rows))

    kv_drain([(last, None)])
    for n in range(outs):
        out_cross(n, core).wait_send()
        out_cross(n, 1 - core).wait_recv()


def body(pipes, ctxs, tokens, queries, key_weight, value_weight, block_order):
    rows, width = tokens.shape[1:]
    deep, kv_width = key_weight.shape
    per = kv_width // HEAD_SIZE // 2
    pieces = 2 * per
    seq = rows * ctxs
    half = seq // block_order.shape[0]
    query_heads = queries.shape[2] // HEAD_SIZE // 2
    lines = ctxs // 2
    chip_rows = 2 * rows
    dma = pltpu.SemaphoreType.DMA
    any_space = pl.BlockSpec(memory_space=pl.ANY)
    return pl.pallas_call(
        functools.partial(kernel, pipes, ctxs, half),
        out_shape=pltpu.VMEM(queries.shape, jnp.bfloat16),
        in_specs=[any_space] * 4 + [pl.BlockSpec(memory_space=pltpu.SMEM)],
        out_specs=pl.BlockSpec(memory_space=pltpu.VMEM),
        scratch_shapes=[
            pltpu.VMEM((2, deep * ctxs, per * HEAD_SIZE), jnp.bfloat16),
            pltpu.VMEM((pipes, 2, 2, rows // 2, width // pipes), jnp.bfloat16),
            pltpu.VMEM((pieces, pipes, 2, rows, HEAD_SIZE), PARTIAL),
            pltpu.VMEM((pieces, pipes - 1, 2, rows, HEAD_SIZE), PARTIAL),
            pltpu.VMEM((pieces, 2, rows, HEAD_SIZE), jnp.float32),
            pltpu.VMEM((pieces, lines, 2, rows, HEAD_SIZE), jnp.bfloat16),
            pltpu.VMEM((chip_rows, queries.shape[2] // 2), jnp.bfloat16),
            pltpu.VMEM((chip_rows, seq), jnp.float32),
            pltpu.VMEM((query_heads, chip_rows, seq), jnp.bfloat16),
            pltpu.VMEM((query_heads, chip_rows, 1), jnp.float32),
            pltpu.VMEM((rows, queries.shape[2] // 2), jnp.bfloat16),
            dma((pieces, ctxs, 2)),
            dma((pieces, ctxs)),
            dma((pieces,)),
            dma((pieces, 2, lines, 2)),
            dma((pieces, 2, lines)),
            dma((pipes - 1, 2, TOKEN_PARTS)),
            dma((pipes - 1, 2, TOKEN_PARTS)),
            dma((pipes - 1, 2, TOKEN_PARTS)),
            dma((pipes - 1, 2, TOKEN_PARTS)),
            dma((2,)),
            dma((2,)),
            dma((pieces, 2, pipes - 1)),
            dma((pieces, 2, pipes - 1)),
            dma((2,)),
            dma((2 * per,)),
            dma((2 * per,)),
            dma((pieces + 3,)),
        ],
        compiler_params=pltpu.CompilerParams(
            collective_id=0, has_side_effects=True, vmem_limit_bytes=VMEM_LIMIT
        ),
    )(tokens, queries, key_weight, value_weight, block_order)


def solution(mesh):
    return jax.shard_map(
        functools.partial(body, mesh.shape["pipe"], mesh.shape["ctx"]),
        mesh=mesh,
        in_specs=(
            P("pipe", "ctx", None),
            P("pipe", "ctx", None),
            P(("pipe", "ctx"), None),
            P(("pipe", "ctx"), None),
            P(),
        ),
        out_specs=P("pipe", "ctx", None),
        check_vma=False,
    )
```

```python
import functools

import jax
import jax.numpy as jnp
from jax import lax
from jax.experimental import pallas as pl
from jax.experimental.pallas import tpu as pltpu
from jax.sharding import PartitionSpec as P

HEAD_SIZE = 128
LOG2E = 1.4426950408889634
MESH = pl.DeviceIdType.MESH
PARTIAL = jnp.bfloat16
TOKEN_PARTS = 2
VMEM_LIMIT = 60 * 1024 * 1024


def block_at(index, size):
    return pl.ds(pl.multiple_of(index * size, size), size)


def remote(src, dst, send_sem, recv_sem, device_id):
    return pltpu.make_async_remote_copy(
        src_ref=src, dst_ref=dst, send_sem=send_sem, recv_sem=recv_sem, device_id=device_id, device_id_type=MESH
    )


def kernel(
    pipes, ctxs, half,
    tok, qry, kw, vw, order, out,
    wbuf, xbuf, pout, pin, mine, kvbuf, qbuf, cap, pbuf, abuf, obuf,
    w_send, w_recv, w_cross, kv_send, kv_recv, x_send, x_recv, xr_send, xr_recv, xo_send, xo_recv,
    p_send, p_recv, q_sem, o_send, o_recv, local,
):
    rows = 2 * xbuf.shape[3]
    small = xbuf.shape[3]
    slice_rows = xbuf.shape[4]
    parts = x_send.shape[2]
    part_rows = slice_rows // parts
    deep = kw.shape[0]
    lines = ctxs // 2
    heads = kw.shape[1] // HEAD_SIZE
    per = heads // 2
    pieces = 2 * per
    group = qbuf.shape[1] // (per * HEAD_SIZE)
    chip_rows = 2 * rows
    seq = ctxs * rows
    half_columns = qbuf.shape[1]
    pipe = lax.axis_index("pipe")
    me = lax.axis_index("ctx")
    line = me // 2
    core = me % 2
    partner = me + 1 - 2 * core


    def weight_source(j, to_core):
        return (kw, vw)[j // per].at[:, block_at(to_core * per + j % per, HEAD_SIZE)]

    def weight_block(j, origin):
        return wbuf.at[j // per, block_at(origin, deep), pl.ds(j % per * HEAD_SIZE, HEAD_SIZE)]

    def weight_local(j):
        return pltpu.make_async_copy(weight_source(j, core), weight_block(j, me), local.at[j])

    def weight_cross(j):
        return remote(
            weight_source(j, 1 - core), weight_block(j, me), w_cross.at[j], w_recv.at[j, me], {"ctx": partner}
        )

    def weight_copy(j, origin, way):
        block = weight_block(j, origin)
        return remote(
            block, block, w_send.at[j, origin, way], w_recv.at[j, origin], {"ctx": (me + 2, me - 2)[way]}
        )

    def weight_spread(j, origin):
        @pl.when(line < lines - 1)
        def _():
            weight_copy(j, origin, 0).start()

        @pl.when(line > 0)
        def _():
            weight_copy(j, origin, 1).start()

    def weight_own(j):
        weight_local(j).wait()
        weight_spread(j, me)
        weight_copy(j, partner, 0).wait_recv()
        weight_spread(j, partner)

    def weight_forward(j, hop):
        @pl.when((line >= hop) & (line < lines - 1))
        def _():
            for sub in range(2):
                origin = 2 * (line - hop) + sub
                weight_copy(j, origin, 0).wait_recv()
                weight_copy(j, origin, 0).start()

        @pl.when((line + hop < lines) & (line > 0))
        def _():
            for sub in range(2):
                origin = 2 * (line + hop) + sub
                weight_copy(j, origin, 1).wait_recv()
                weight_copy(j, origin, 1).start()

    def weight_join(j):
        @pl.when((line == 0) | (line == lines - 1))
        def _():
            @pl.loop(1, lines)
            def _(hop):
                for sub in range(2):
                    origin = 2 * jnp.where(line == 0, hop, lines - 1 - hop) + sub
                    weight_copy(j, origin, 0).wait_recv()


    def token_slice(index, m, part):
        columns = pl.ds(pl.multiple_of(index * slice_rows + part * part_rows, part_rows), part_rows)
        return tok.at[0, pl.ds(m * small, small), columns]

    def token_block(index, m, owner, part):
        return xbuf.at[index, m, owner, :, pl.ds(part * part_rows, part_rows)]

    def token_own(m):
        return tok.at[0, pl.ds(m * small, small), block_at(pipe, slice_rows)]

    def token_local(m):
        return pltpu.make_async_copy(token_own(m), xbuf.at[pipe, m, core], local.at[pieces + m])

    def token_cross(m, owner):
        return remote(token_own(m), xbuf.at[pipe, m, owner], xo_send.at[m], xo_recv.at[m], {"ctx": partner})

    def token_copy(d, m, part):
        to = lax.rem(pipe + d, pipes)
        return remote(
            token_slice(to, m, part), token_block(pipe, m, core, part),
            x_send.at[d - 1, m, part], x_recv.at[d - 1, m, part], {"pipe": to},
        )

    def token_relay(d, m, owner, part):
        block = token_block(lax.rem(pipe + pipes - d, pipes), m, owner, part)
        return remote(block, block, xr_send.at[d - 1, m, part], xr_recv.at[d - 1, m, part], {"ctx": partner})

    def token_arrived(d, m, part):
        block = token_block(lax.rem(pipe + pipes - d, pipes), m, core, part)
        to = lax.rem(pipe + d, pipes)
        remote(
            block, block, x_send.at[d - 1, m, part], x_recv.at[d - 1, m, part], {"pipe": to}
        ).wait_recv()


    def query_local():
        return pltpu.make_async_copy(
            qry.at[0, :, block_at(core, half_columns)], qbuf.at[pl.ds(0, rows)], local.at[pieces + 2]
        )

    def query_cross():
        return remote(
            qry.at[0, :, block_at(1 - core, half_columns)],
            qbuf.at[pl.ds(rows, rows)], q_sem.at[0], q_sem.at[1], {"ctx": partner},
        )


    def rows_of(m):
        return pl.ds(0, 2) if m is None else pl.ds(m, 1)

    def partial_copy(j, m, d):
        to = lax.rem(pipe + d, pipes)
        return remote(
            pout.at[j, to, rows_of(m)], pin.at[j, d - 1, rows_of(m)],
            p_send.at[j, m or 0, d - 1], p_recv.at[j, m or 0, d - 1], {"pipe": to},
        )

    def multiply(which, first, stop, m):
        columns = slice(first * HEAD_SIZE, stop * HEAD_SIZE)
        count = 2 if m is None else 1
        place = slice(0, 2) if m is None else slice(m, m + 1)

        def product(index):
            left = xbuf[index, place].reshape(count * rows, slice_rows)
            return jnp.dot(left, wbuf[which, :, columns], preferred_element_type=jnp.float32)

        def part_of(value, h):
            value = value[:, (h - first) * HEAD_SIZE : (h - first + 1) * HEAD_SIZE]
            return value.reshape(count, rows, HEAD_SIZE)

        @pl.loop(1, pipes)
        def _(d):
            to = lax.rem(pipe + d, pipes)
            value = product(to)
            for h in range(first, stop):
                pout[which * per + h, to, place] = part_of(value, h).astype(pout.dtype)
            partial_copy(which * per + first, m, d).start()

        for h in range(first + 1, stop):
            for d in range(1, pipes):
                partial_copy(which * per + h, m, d).start()

        value = product(pipe)
        for h in range(first, stop):
            mine[which * per + h, place] = part_of(value, h)


    def kv_copy(j, m, origin, way):
        block = kvbuf.at[j, origin, rows_of(m)]
        return remote(
            block, block, kv_send.at[j, m or 0, origin, way], kv_recv.at[j, m or 0, origin],
            {"ctx": (me + 2, me - 2)[way]},
        )

    def total(j, m):
        place = slice(0, 2) if m is None else slice(m, m + 1)
        value = mine[j, place]
        for d in range(1, pipes):
            partial_copy(j, m, d).wait_recv()
            value = value + pin[j, d - 1, place].astype(jnp.float32)
        kvbuf[j, line, place] = value.astype(jnp.bfloat16)

        @pl.when(line < lines - 1)
        def _():
            kv_copy(j, m, line, 0).start()

        @pl.when(line > 0)
        def _():
            kv_copy(j, m, line, 1).start()

    def kv_forward(j, m, first, stop):
        @pl.loop(first, stop)
        def _(hop):
            @pl.when((line >= hop) & (line < lines - 1))
            def _():
                kv_copy(j, m, line - hop, 0).wait_recv()
                kv_copy(j, m, line - hop, 0).start()

            @pl.when((line + hop < lines) & (line > 0))
            def _():
                kv_copy(j, m, line + hop, 1).wait_recv()
                kv_copy(j, m, line + hop, 1).start()

    def kv_join(j, m, first=1, stop=None):
        @pl.when((line == 0) | (line == lines - 1))
        def _():
            @pl.loop(first, lines if stop is None else stop)
            def _(hop):
                kv_copy(j, m, jnp.where(line == 0, hop, lines - 1 - hop), 0).wait_recv()


    factor = LOG2E / HEAD_SIZE**0.5
    outs = o_send.shape[0]
    out_columns = half_columns // outs
    middle = max(lines // 2, 2)

    def head_columns(head):
        return block_at(head, HEAD_SIZE)

    def soften(h, i):
        head = h * group + i
        score = lax.dot_general(
            qbuf[:, head_columns(head)], kvbuf[h].reshape(seq, HEAD_SIZE), (((1,), (1,)), ((), ())), preferred_element_type=jnp.float32
        )
        score = jnp.minimum(score, cap[...])
        largest = jnp.max(score, axis=1, keepdims=True)
        expo = jnp.exp2((score - largest) * factor)
        return expo.astype(jnp.bfloat16), jnp.sum(expo, axis=1, keepdims=True)

    def values_of(h, first, count):
        return kvbuf[per + h, pl.ds(first, count)].reshape(count * chip_rows, HEAD_SIZE)

    def own_out(h, i):
        return out.at[0, :, head_columns(core * per * group + h * group + i)]

    def finish(h, i):
        head = h * group + i
        summed = jnp.dot(pbuf[head], values_of(h, 0, lines), preferred_element_type=jnp.float32)
        value = (summed / abuf[head]).astype(jnp.bfloat16)
        own_out(h, i)[...] = value[:rows]
        obuf[:, head_columns(head)] = value[rows:]


    def finish_far(h, i, place):
        summed = jnp.dot(pbuf[h * group + i, place], values_of(h, 0, lines), preferred_element_type=jnp.float32)
        return (summed / abuf[h * group + i, place]).astype(jnp.bfloat16)

    def out_cross(n, owner):
        return remote(
            obuf.at[:, pl.ds(n * out_columns, out_columns)],
            out.at[0, :, block_at(owner * outs + n, out_columns)],
            o_send.at[n], o_recv.at[n], {"ctx": partner},
        )


    for j in range(pieces):
        weight_local(j).start()
    for m in range(2):
        token_local(m).start()
    query_local().start()

    barrier = pltpu.get_barrier_semaphore()
    for d in range(1, pipes):
        pl.semaphore_signal(barrier, inc=1, device_id={"pipe": lax.rem(pipe + d, pipes)}, device_id_type=MESH)
    pl.semaphore_signal(barrier, inc=1, device_id={"ctx": partner}, device_id_type=MESH)

    @pl.when(line < lines - 1)
    def _():
        pl.semaphore_signal(barrier, inc=1, device_id={"ctx": me + 2}, device_id_type=MESH)

    @pl.when(line > 0)
    def _():
        pl.semaphore_signal(barrier, inc=1, device_id={"ctx": me - 2}, device_id_type=MESH)

    pl.semaphore_wait(barrier, pipes + (line > 0).astype(jnp.int32) + (line < lines - 1).astype(jnp.int32))

    for j in range(pieces):
        weight_cross(j).start()
    weight_own(0)
    for m in range(2):
        for part in range(parts):
            for d in range(1, pipes):
                token_copy(d, m, part).start()
    weight_own(1)
    for m in range(2):
        token_cross(m, core).start()
    query_cross().start()

    lane = lax.broadcasted_iota(jnp.int32, (1, seq), 1)
    inside = lane % chip_rows
    lane = (lane // chip_rows) * chip_rows + inside % rows // small * rows + inside // rows * small + lane % small
    spot = jnp.zeros((1, seq), jnp.int32)
    for i in range(seq // half):
        spot = jnp.where(lane // half == i, order[i] * half, spot)
    key_position = spot + lane % half
    row = lax.broadcasted_iota(jnp.int32, (chip_rows, 1), 0)
    row = jnp.where(row < rows, row + core * rows, row - core * rows)
    spot = jnp.zeros((chip_rows, 1), jnp.int32)
    per_line = chip_rows // half
    for i in range(per_line):
        spot = jnp.where(row // half == i, order[line * per_line + i] * half, spot)
    own_position = spot + row % half
    cap[...] = jnp.where(key_position <= own_position, jnp.inf, -jnp.inf)

    def tokens_ready(m):
        token_local(m).wait()
        for part in range(parts):
            for d in range(1, pipes):
                token_arrived(d, m, part)
                token_relay(d, m, core, part).start()
        token_cross(m, 1 - core).wait_recv()
        for part in range(parts):
            for d in range(1, pipes):
                token_relay(d, m, 1 - core, part).wait_recv()

    def weight_steps(first, stop):
        for step in range(first, stop):
            for hop in range(lines - 2, 0, -1):
                if 0 <= step - hop + 1 < pieces:
                    weight_forward(step - hop + 1, hop)
            if step + 2 < pieces:
                weight_own(step + 2)

    keys = range(per)
    last = pieces - 1
    weight_steps(0, per + lines - 3)
    tokens_ready(0)
    for j in keys:
        weight_join(j)
    multiply(0, 0, per, 0)
    weight_steps(per + lines - 3, pieces + lines - 3)
    tokens_ready(1)
    multiply(0, 0, per, 1)
    for j in keys:
        total(j, 0)
    for j in range(per, last):
        weight_join(j)
        multiply(1, j - per, j - per + 1, None)

    @pl.when((line > 0) & (line < lines - 1))
    def _():
        multiply(1, per - 1, per, None)

    for j in keys:
        kv_forward(j, 0, 1, middle)
    for j in keys:
        total(j, 1)
    for j in keys:
        kv_forward(j, 0, middle, lines - 1)

    @pl.when((line == 0) | (line == lines - 1))
    def _():
        weight_join(last)
        multiply(1, per - 1, per, None)

    for j in keys:
        kv_forward(j, 1, 1, middle)
    for j in range(per, last):
        total(j, None)
    for j in keys:
        kv_forward(j, 1, middle, lines - 1)
    total(last, None)

    def weights_drain():
        @pl.loop(0, lines)
        def _(other):
            for j in range(pieces):
                for sub in range(2):
                    origin = 2 * other + sub

                    @pl.when((other <= line) & (line < lines - 1))
                    def _():
                        weight_copy(j, origin, 0).wait_send()

                    @pl.when((other >= line) & (line > 0))
                    def _():
                        weight_copy(j, origin, 1).wait_send()

        for j in range(pieces):
            weight_cross(j).wait_send()

    def others_drain():
        query_cross().wait_send()
        for m in range(2):
            token_cross(m, core).wait_send()
        for d in range(1, pipes):
            for m in range(2):
                for part in range(parts):
                    token_copy(d, m, part).wait_send()
                    token_relay(d, m, core, part).wait_send()
                for j in keys:
                    partial_copy(j, m, d).wait_send()
            for j in range(per, pieces):
                partial_copy(j, None, d).wait_send()

    def soft_group(h, first, stop):
        @pl.loop(first, stop, unroll=4)
        def _(i):
            weight, amount = soften(h, i)
            pbuf[h * group + i] = weight
            abuf[h * group + i] = amount

    def finish_group(h, first, stop):
        @pl.loop(first, stop, unroll=4)
        def _(i):
            finish(h, i)

    query_local().wait()
    query_cross().wait_recv()
    some = group // 2
    for j in range(per, last):
        kv_forward(j, None, 1, middle)
    weights_drain()
    others_drain()
    for h in keys:
        kv_join(h, 0)
        kv_join(h, 1)
        soft_group(h, 0, some)
        if h == 0:
            for j in range(per, last):
                kv_forward(j, None, middle, lines - 1)
            kv_forward(last, None, 1, middle)
        if h == per - 1:
            kv_forward(last, None, middle, lines - 1)
        soft_group(h, some, group)
    def kv_drain(units):
        @pl.loop(0, lines)
        def _(other):
            for j, m in units:

                @pl.when((other <= line) & (line < lines - 1))
                def _():
                    kv_copy(j, m, other, 0).wait_send()

                @pl.when((other >= line) & (line > 0))
                def _():
                    kv_copy(j, m, other, 1).wait_send()

    for h in range(per - 1):
        kv_join(per + h, None)
        for part in range(outs // per):
            finish_group(h, part * group * per // outs, (part + 1) * group * per // outs)
            out_cross(h * outs // per + part, core).start()
    kv_drain([(j, m) for j in keys for m in range(2)] + [(j, None) for j in range(per, last)])
    kv_join(last, None)

    @pl.loop(0, group, unroll=8)
    def _(i):
        obuf[:, head_columns((per - 1) * group + i)] = finish_far(per - 1, i, slice(rows, chip_rows))

    for n in range(outs - outs // per, outs):
        out_cross(n, core).start()

    @pl.loop(0, group, unroll=8)
    def _(i):
        own_out(per - 1, i)[...] = finish_far(per - 1, i, slice(0, rows))

    kv_drain([(last, None)])
    for n in range(outs):
        out_cross(n, core).wait_send()
        out_cross(n, 1 - core).wait_recv()


def body(pipes, ctxs, tokens, queries, key_weight, value_weight, block_order):
    rows, width = tokens.shape[1:]
    deep, kv_width = key_weight.shape
    per = kv_width // HEAD_SIZE // 2
    pieces = 2 * per
    seq = rows * ctxs
    half = seq // block_order.shape[0]
    query_heads = queries.shape[2] // HEAD_SIZE // 2
    lines = ctxs // 2
    chip_rows = 2 * rows
    dma = pltpu.SemaphoreType.DMA
    any_space = pl.BlockSpec(memory_space=pl.ANY)
    return pl.pallas_call(
        functools.partial(kernel, pipes, ctxs, half),
        out_shape=pltpu.VMEM(queries.shape, jnp.bfloat16),
        in_specs=[any_space] * 4 + [pl.BlockSpec(memory_space=pltpu.SMEM)],
        out_specs=pl.BlockSpec(memory_space=pltpu.VMEM),
        scratch_shapes=[
            pltpu.VMEM((2, deep * ctxs, per * HEAD_SIZE), jnp.bfloat16),
            pltpu.VMEM((pipes, 2, 2, rows // 2, width // pipes), jnp.bfloat16),
            pltpu.VMEM((pieces, pipes, 2, rows, HEAD_SIZE), PARTIAL),
            pltpu.VMEM((pieces, pipes - 1, 2, rows, HEAD_SIZE), PARTIAL),
            pltpu.VMEM((pieces, 2, rows, HEAD_SIZE), jnp.float32),
            pltpu.VMEM((pieces, lines, 2, rows, HEAD_SIZE), jnp.bfloat16),
            pltpu.VMEM((chip_rows, queries.shape[2] // 2), jnp.bfloat16),
            pltpu.VMEM((chip_rows, seq), jnp.float32),
            pltpu.VMEM((query_heads, chip_rows, seq), jnp.bfloat16),
            pltpu.VMEM((query_heads, chip_rows, 1), jnp.float32),
            pltpu.VMEM((rows, queries.shape[2] // 2), jnp.bfloat16),
            dma((pieces, ctxs, 2)),
            dma((pieces, ctxs)),
            dma((pieces,)),
            dma((pieces, 2, lines, 2)),
            dma((pieces, 2, lines)),
            dma((pipes - 1, 2, TOKEN_PARTS)),
            dma((pipes - 1, 2, TOKEN_PARTS)),
            dma((pipes - 1, 2, TOKEN_PARTS)),
            dma((pipes - 1, 2, TOKEN_PARTS)),
            dma((2,)),
            dma((2,)),
            dma((pieces, 2, pipes - 1)),
            dma((pieces, 2, pipes - 1)),
            dma((2,)),
            dma((2 * per,)),
            dma((2 * per,)),
            dma((pieces + 3,)),
        ],
        compiler_params=pltpu.CompilerParams(
            collective_id=0, has_side_effects=True, vmem_limit_bytes=VMEM_LIMIT
        ),
    )(tokens, queries, key_weight, value_weight, block_order)


def solution(mesh):
    return jax.shard_map(
        functools.partial(body, mesh.shape["pipe"], mesh.shape["ctx"]),
        mesh=mesh,
        in_specs=(
            P("pipe", "ctx", None),
            P("pipe", "ctx", None),
            P(("pipe", "ctx"), None),
            P(("pipe", "ctx"), None),
            P(),
        ),
        out_specs=P("pipe", "ctx", None),
        check_vma=False,
    )
```

```python
import functools

import jax
import jax.numpy as jnp
from jax import lax
from jax.experimental import pallas as pl
from jax.experimental.pallas import tpu as pltpu
from jax.sharding import PartitionSpec as P

HEAD_SIZE = 128
LOG2E = 1.4426950408889634
MESH = pl.DeviceIdType.MESH
PARTIAL = jnp.bfloat16
TOKEN_PARTS = 2
VMEM_LIMIT = 60 * 1024 * 1024


def block_at(index, size, count=1):
    return pl.ds(pl.multiple_of(index * size, size), size * count)


def remote(src, dst, send_sem, recv_sem, device_id):
    return pltpu.make_async_remote_copy(
        src_ref=src, dst_ref=dst, send_sem=send_sem, recv_sem=recv_sem, device_id=device_id, device_id_type=MESH
    )


def kernel(
    pipes, ctxs, half,
    tok, qry, kw, vw, order, out,
    wbuf, xbuf, pout, pin, mine, kvbuf, qbuf, cap, pbuf, abuf, obuf,
    w_send, w_recv, w_cross, kv_send, kv_recv, x_send, x_recv, xr_send, xr_recv, xo_send, xo_recv,
    p_send, p_recv, q_sem, o_send, o_recv, local,
):
    rows = 2 * xbuf.shape[3]
    small = xbuf.shape[3]
    slice_rows = xbuf.shape[4]
    parts = x_send.shape[2]
    part_rows = slice_rows // parts
    deep = kw.shape[0]
    lines = ctxs // 2
    heads = kw.shape[1] // HEAD_SIZE
    per = heads // 2
    pieces = 2 * per
    group = qbuf.shape[1] // (per * HEAD_SIZE)
    chip_rows = 2 * rows
    seq = ctxs * rows
    half_columns = qbuf.shape[1]
    pipe = lax.axis_index("pipe")
    me = lax.axis_index("ctx")
    line = me // 2
    core = me % 2
    partner = me + 1 - 2 * core


    def weight_source(j, to_core):
        return (kw, vw)[j // per].at[:, block_at(to_core * per + j % per, HEAD_SIZE)]

    def weight_block(j, origin):
        return wbuf.at[j // per, block_at(origin, deep), pl.ds(j % per * HEAD_SIZE, HEAD_SIZE)]

    def weight_local(j):
        return pltpu.make_async_copy(weight_source(j, core), weight_block(j, me), local.at[j])

    def weight_cross(j):
        return remote(
            weight_source(j, 1 - core), weight_block(j, me), w_cross.at[j], w_recv.at[j, me], {"ctx": partner}
        )

    def weight_copy(j, origin, way):
        block = weight_block(j, origin)
        return remote(
            block, block, w_send.at[j, origin, way], w_recv.at[j, origin], {"ctx": (me + 2, me - 2)[way]}
        )

    def weight_spread(j, origin):
        @pl.when(line < lines - 1)
        def _():
            weight_copy(j, origin, 0).start()

        @pl.when(line > 0)
        def _():
            weight_copy(j, origin, 1).start()

    def weight_own(j):
        weight_local(j).wait()
        weight_spread(j, me)
        weight_copy(j, partner, 0).wait_recv()
        weight_spread(j, partner)

    def weight_forward(j, hop):
        @pl.when((line >= hop) & (line < lines - 1))
        def _():
            for sub in range(2):
                origin = 2 * (line - hop) + sub
                weight_copy(j, origin, 0).wait_recv()
                weight_copy(j, origin, 0).start()

        @pl.when((line + hop < lines) & (line > 0))
        def _():
            for sub in range(2):
                origin = 2 * (line + hop) + sub
                weight_copy(j, origin, 1).wait_recv()
                weight_copy(j, origin, 1).start()

    def weight_join(j):
        @pl.when((line == 0) | (line == lines - 1))
        def _():
            @pl.loop(1, lines)
            def _(hop):
                for sub in range(2):
                    origin = 2 * jnp.where(line == 0, hop, lines - 1 - hop) + sub
                    weight_copy(j, origin, 0).wait_recv()


    def token_slice(index, m, part):
        columns = pl.ds(pl.multiple_of(index * slice_rows + part * part_rows, part_rows), part_rows)
        return tok.at[0, pl.ds(m * small, small), columns]

    def token_block(index, m, owner, part):
        return xbuf.at[index, m, owner, :, pl.ds(part * part_rows, part_rows)]

    def token_own(m):
        return tok.at[0, pl.ds(m * small, small), block_at(pipe, slice_rows)]

    def token_local(m):
        return pltpu.make_async_copy(token_own(m), xbuf.at[pipe, m, core], local.at[pieces + m])

    def token_cross(m, owner):
        return remote(token_own(m), xbuf.at[pipe, m, owner], xo_send.at[m], xo_recv.at[m], {"ctx": partner})

    def token_copy(d, m, part):
        to = lax.rem(pipe + d, pipes)
        return remote(
            token_slice(to, m, part), token_block(pipe, m, core, part),
            x_send.at[d - 1, m, part], x_recv.at[d - 1, m, part], {"pipe": to},
        )

    def token_relay(d, m, owner, part):
        block = token_block(lax.rem(pipe + pipes - d, pipes), m, owner, part)
        return remote(block, block, xr_send.at[d - 1, m, part], xr_recv.at[d - 1, m, part], {"ctx": partner})

    def token_arrived(d, m, part):
        block = token_block(lax.rem(pipe + pipes - d, pipes), m, core, part)
        to = lax.rem(pipe + d, pipes)
        remote(
            block, block, x_send.at[d - 1, m, part], x_recv.at[d - 1, m, part], {"pipe": to}
        ).wait_recv()


    def query_local():
        return pltpu.make_async_copy(
            qry.at[0, :, block_at(core, half_columns)], qbuf.at[pl.ds(0, rows)], local.at[pieces + 2]
        )

    def query_cross():
        return remote(
            qry.at[0, :, block_at(1 - core, half_columns)],
            qbuf.at[pl.ds(rows, rows)], q_sem.at[0], q_sem.at[1], {"ctx": partner},
        )


    def rows_of(m):
        return pl.ds(0, 2) if m is None else pl.ds(m, 1)

    def partial_copy(j, m, d):
        to = lax.rem(pipe + d, pipes)
        return remote(
            pout.at[j, to, rows_of(m)], pin.at[j, d - 1, rows_of(m)],
            p_send.at[j, m or 0, d - 1], p_recv.at[j, m or 0, d - 1], {"pipe": to},
        )

    def multiply(which, first, stop, m):
        columns = slice(first * HEAD_SIZE, stop * HEAD_SIZE)
        count = 2 if m is None else 1
        place = slice(0, 2) if m is None else slice(m, m + 1)

        def product(index):
            left = xbuf[index, place].reshape(count * rows, slice_rows)
            return jnp.dot(left, wbuf[which, :, columns], preferred_element_type=jnp.float32)

        def part_of(value, h):
            value = value[:, (h - first) * HEAD_SIZE : (h - first + 1) * HEAD_SIZE]
            return value.reshape(count, rows, HEAD_SIZE)

        @pl.loop(1, pipes)
        def _(d):
            to = lax.rem(pipe + d, pipes)
            value = product(to)
            for h in range(first, stop):
                pout[which * per + h, to, place] = part_of(value, h).astype(pout.dtype)
            partial_copy(which * per + first, m, d).start()

        for h in range(first + 1, stop):
            for d in range(1, pipes):
                partial_copy(which * per + h, m, d).start()

        value = product(pipe)
        for h in range(first, stop):
            mine[which * per + h, place] = part_of(value, h)


    def kv_copy(j, m, origin, way):
        block = kvbuf.at[j, origin, rows_of(m)]
        return remote(
            block, block, kv_send.at[j, m or 0, origin, way], kv_recv.at[j, m or 0, origin],
            {"ctx": (me + 2, me - 2)[way]},
        )

    def total(j, m):
        place = slice(0, 2) if m is None else slice(m, m + 1)
        value = mine[j, place]
        for d in range(1, pipes):
            partial_copy(j, m, d).wait_recv()
            value = value + pin[j, d - 1, place].astype(jnp.float32)
        kvbuf[j, line, place] = value.astype(jnp.bfloat16)

        @pl.when(line < lines - 1)
        def _():
            kv_copy(j, m, line, 0).start()

        @pl.when(line > 0)
        def _():
            kv_copy(j, m, line, 1).start()

    def kv_forward(j, m, first, stop):
        @pl.loop(first, stop)
        def _(hop):
            @pl.when((line >= hop) & (line < lines - 1))
            def _():
                kv_copy(j, m, line - hop, 0).wait_recv()
                kv_copy(j, m, line - hop, 0).start()

            @pl.when((line + hop < lines) & (line > 0))
            def _():
                kv_copy(j, m, line + hop, 1).wait_recv()
                kv_copy(j, m, line + hop, 1).start()

    def kv_join(j, m, first=1, stop=None):
        @pl.when((line == 0) | (line == lines - 1))
        def _():
            @pl.loop(first, lines if stop is None else stop)
            def _(hop):
                kv_copy(j, m, jnp.where(line == 0, hop, lines - 1 - hop), 0).wait_recv()


    factor = LOG2E / HEAD_SIZE**0.5
    outs = o_send.shape[0]
    out_columns = half_columns // outs
    middle = max(lines // 2, 2)

    def head_columns(head):
        return block_at(head, HEAD_SIZE)

    def soften(h, i):
        head = h * group + i
        score = lax.dot_general(
            qbuf[:, head_columns(head)], kvbuf[h].reshape(seq, HEAD_SIZE), (((1,), (1,)), ((), ())), preferred_element_type=jnp.float32
        )
        score = jnp.minimum(score, cap[...])
        largest = jnp.max(score, axis=1, keepdims=True)
        expo = jnp.exp2((score - largest) * factor)
        return expo.astype(jnp.bfloat16), jnp.sum(expo, axis=1, keepdims=True)

    def values_of(h, first, count):
        return kvbuf[per + h, pl.ds(first, count)].reshape(count * chip_rows, HEAD_SIZE)

    def own_out(h, i):
        return out.at[0, :, head_columns(core * per * group + h * group + i)]

    def finish(h, i):
        head = h * group + i
        summed = jnp.dot(pbuf[head], values_of(h, 0, lines), preferred_element_type=jnp.float32)
        value = (summed / abuf[head]).astype(jnp.bfloat16)
        own_out(h, i)[...] = value[:rows]
        obuf[:, head_columns(head)] = value[rows:]


    near = line // (lines // 2) * (lines // 2)

    def product_of(h, i, place, first):
        weight = pbuf[h * group + i, place, block_at(first, chip_rows, lines // 2)]
        return jnp.dot(weight, values_of(h, first, lines // 2), preferred_element_type=jnp.float32)

    def finish_near(h, i):
        cap[:, head_columns(i)] = product_of(h, i, slice(0, chip_rows), near)

    def finish_far(h, i, place):
        summed = cap[place, head_columns(i)] + product_of(h, i, place, lines // 2 - near)
        return (summed / abuf[h * group + i, place]).astype(jnp.bfloat16)

    def out_cross(n, owner):
        return remote(
            obuf.at[:, pl.ds(n * out_columns, out_columns)],
            out.at[0, :, block_at(owner * outs + n, out_columns)],
            o_send.at[n], o_recv.at[n], {"ctx": partner},
        )


    for j in range(pieces):
        weight_local(j).start()
    for m in range(2):
        token_local(m).start()
    query_local().start()

    barrier = pltpu.get_barrier_semaphore()
    for d in range(1, pipes):
        pl.semaphore_signal(barrier, inc=1, device_id={"pipe": lax.rem(pipe + d, pipes)}, device_id_type=MESH)
    pl.semaphore_signal(barrier, inc=1, device_id={"ctx": partner}, device_id_type=MESH)

    @pl.when(line < lines - 1)
    def _():
        pl.semaphore_signal(barrier, inc=1, device_id={"ctx": me + 2}, device_id_type=MESH)

    @pl.when(line > 0)
    def _():
        pl.semaphore_signal(barrier, inc=1, device_id={"ctx": me - 2}, device_id_type=MESH)

    pl.semaphore_wait(barrier, pipes + (line > 0).astype(jnp.int32) + (line < lines - 1).astype(jnp.int32))

    for j in range(pieces):
        weight_cross(j).start()
    weight_own(0)
    for m in range(2):
        for part in range(parts):
            for d in range(1, pipes):
                token_copy(d, m, part).start()
    weight_own(1)
    for m in range(2):
        token_cross(m, core).start()
    query_cross().start()

    lane = lax.broadcasted_iota(jnp.int32, (1, seq), 1)
    inside = lane % chip_rows
    lane = (lane // chip_rows) * chip_rows + inside % rows // small * rows + inside // rows * small + lane % small
    spot = jnp.zeros((1, seq), jnp.int32)
    for i in range(seq // half):
        spot = jnp.where(lane // half == i, order[i] * half, spot)
    key_position = spot + lane % half
    row = lax.broadcasted_iota(jnp.int32, (chip_rows, 1), 0)
    row = jnp.where(row < rows, row + core * rows, row - core * rows)
    spot = jnp.zeros((chip_rows, 1), jnp.int32)
    per_line = chip_rows // half
    for i in range(per_line):
        spot = jnp.where(row // half == i, order[line * per_line + i] * half, spot)
    own_position = spot + row % half
    cap[...] = jnp.where(key_position <= own_position, jnp.inf, -jnp.inf)

    def tokens_ready(m):
        token_local(m).wait()
        for part in range(parts):
            for d in range(1, pipes):
                token_arrived(d, m, part)
                token_relay(d, m, core, part).start()
        token_cross(m, 1 - core).wait_recv()
        for part in range(parts):
            for d in range(1, pipes):
                token_relay(d, m, 1 - core, part).wait_recv()

    def weight_steps(first, stop):
        for step in range(first, stop):
            for hop in range(lines - 2, 0, -1):
                if 0 <= step - hop + 1 < pieces:
                    weight_forward(step - hop + 1, hop)
            if step + 2 < pieces:
                weight_own(step + 2)

    keys = range(per)
    last = pieces - 1
    weight_steps(0, per + lines - 3)
    tokens_ready(0)
    for j in keys:
        weight_join(j)
    multiply(0, 0, per, 0)
    weight_steps(per + lines - 3, pieces + lines - 3)
    tokens_ready(1)
    multiply(0, 0, per, 1)
    for j in keys:
        total(j, 0)
    for j in range(per, last):
        weight_join(j)
        multiply(1, j - per, j - per + 1, None)

    @pl.when((line > 0) & (line < lines - 1))
    def _():
        multiply(1, per - 1, per, None)

    for j in keys:
        kv_forward(j, 0, 1, middle)
    for j in keys:
        total(j, 1)
    for j in keys:
        kv_forward(j, 0, middle, lines - 1)

    @pl.when((line == 0) | (line == lines - 1))
    def _():
        weight_join(last)
        multiply(1, per - 1, per, None)

    for j in keys:
        kv_forward(j, 1, 1, middle)
    for j in range(per, last):
        total(j, None)
    for j in keys:
        kv_forward(j, 1, middle, lines - 1)
    total(last, None)

    def weights_drain():
        @pl.loop(0, lines)
        def _(other):
            for j in range(pieces):
                for sub in range(2):
                    origin = 2 * other + sub

                    @pl.when((other <= line) & (line < lines - 1))
                    def _():
                        weight_copy(j, origin, 0).wait_send()

                    @pl.when((other >= line) & (line > 0))
                    def _():
                        weight_copy(j, origin, 1).wait_send()

        for j in range(pieces):
            weight_cross(j).wait_send()

    def others_drain():
        query_cross().wait_send()
        for m in range(2):
            token_cross(m, core).wait_send()
        for d in range(1, pipes):
            for m in range(2):
                for part in range(parts):
                    token_copy(d, m, part).wait_send()
                    token_relay(d, m, core, part).wait_send()
                for j in keys:
                    partial_copy(j, m, d).wait_send()
            for j in range(per, pieces):
                partial_copy(j, None, d).wait_send()

    def soft_group(h, first, stop):
        @pl.loop(first, stop, unroll=4)
        def _(i):
            weight, amount = soften(h, i)
            pbuf[h * group + i] = weight
            abuf[h * group + i] = amount

    def finish_group(h, first, stop):
        @pl.loop(first, stop, unroll=4)
        def _(i):
            finish(h, i)

    query_local().wait()
    query_cross().wait_recv()
    some = group // 2
    for j in range(per, last):
        kv_forward(j, None, 1, middle)
    weights_drain()
    others_drain()
    for h in keys:
        kv_join(h, 0)
        kv_join(h, 1)
        soft_group(h, 0, some)
        if h == 0:
            for j in range(per, last):
                kv_forward(j, None, middle, lines - 1)
            kv_forward(last, None, 1, middle)
        if h == per - 1:
            kv_forward(last, None, middle, lines - 1)
        soft_group(h, some, group)
    def kv_drain(units):
        @pl.loop(0, lines)
        def _(other):
            for j, m in units:

                @pl.when((other <= line) & (line < lines - 1))
                def _():
                    kv_copy(j, m, other, 0).wait_send()

                @pl.when((other >= line) & (line > 0))
                def _():
                    kv_copy(j, m, other, 1).wait_send()

    for h in range(per - 1):
        kv_join(per + h, None)
        for part in range(outs // per):
            finish_group(h, part * group * per // outs, (part + 1) * group * per // outs)
            out_cross(h * outs // per + part, core).start()
    kv_drain([(j, m) for j in keys for m in range(2)] + [(j, None) for j in range(per, last)])
    kv_join(last, None, 1, lines // 2)

    @pl.loop(0, group, unroll=8)
    def _(i):
        finish_near(per - 1, i)

    kv_join(last, None, lines // 2)

    @pl.loop(0, group, unroll=8)
    def _(i):
        obuf[:, head_columns((per - 1) * group + i)] = finish_far(per - 1, i, slice(rows, chip_rows))

    for n in range(outs - outs // per, outs):
        out_cross(n, core).start()

    @pl.loop(0, group, unroll=8)
    def _(i):
        own_out(per - 1, i)[...] = finish_far(per - 1, i, slice(0, rows))

    kv_drain([(last, None)])
    for n in range(outs):
        out_cross(n, core).wait_send()
        out_cross(n, 1 - core).wait_recv()


def body(pipes, ctxs, tokens, queries, key_weight, value_weight, block_order):
    rows, width = tokens.shape[1:]
    deep, kv_width = key_weight.shape
    per = kv_width // HEAD_SIZE // 2
    pieces = 2 * per
    seq = rows * ctxs
    half = seq // block_order.shape[0]
    query_heads = queries.shape[2] // HEAD_SIZE // 2
    lines = ctxs // 2
    chip_rows = 2 * rows
    dma = pltpu.SemaphoreType.DMA
    any_space = pl.BlockSpec(memory_space=pl.ANY)
    return pl.pallas_call(
        functools.partial(kernel, pipes, ctxs, half),
        out_shape=pltpu.VMEM(queries.shape, jnp.bfloat16),
        in_specs=[any_space] * 4 + [pl.BlockSpec(memory_space=pltpu.SMEM)],
        out_specs=pl.BlockSpec(memory_space=pltpu.VMEM),
        scratch_shapes=[
            pltpu.VMEM((2, deep * ctxs, per * HEAD_SIZE), jnp.bfloat16),
            pltpu.VMEM((pipes, 2, 2, rows // 2, width // pipes), jnp.bfloat16),
            pltpu.VMEM((pieces, pipes, 2, rows, HEAD_SIZE), PARTIAL),
            pltpu.VMEM((pieces, pipes - 1, 2, rows, HEAD_SIZE), PARTIAL),
            pltpu.VMEM((pieces, 2, rows, HEAD_SIZE), jnp.float32),
            pltpu.VMEM((pieces, lines, 2, rows, HEAD_SIZE), jnp.bfloat16),
            pltpu.VMEM((chip_rows, queries.shape[2] // 2), jnp.bfloat16),
            pltpu.VMEM((chip_rows, seq), jnp.float32),
            pltpu.VMEM((query_heads, chip_rows, seq), jnp.bfloat16),
            pltpu.VMEM((query_heads, chip_rows, 1), jnp.float32),
            pltpu.VMEM((rows, queries.shape[2] // 2), jnp.bfloat16),
            dma((pieces, ctxs, 2)),
            dma((pieces, ctxs)),
            dma((pieces,)),
            dma((pieces, 2, lines, 2)),
            dma((pieces, 2, lines)),
            dma((pipes - 1, 2, TOKEN_PARTS)),
            dma((pipes - 1, 2, TOKEN_PARTS)),
            dma((pipes - 1, 2, TOKEN_PARTS)),
            dma((pipes - 1, 2, TOKEN_PARTS)),
            dma((2,)),
            dma((2,)),
            dma((pieces, 2, pipes - 1)),
            dma((pieces, 2, pipes - 1)),
            dma((2,)),
            dma((2 * per,)),
            dma((2 * per,)),
            dma((pieces + 3,)),
        ],
        compiler_params=pltpu.CompilerParams(
            collective_id=0, has_side_effects=True, vmem_limit_bytes=VMEM_LIMIT
        ),
    )(tokens, queries, key_weight, value_weight, block_order)


def solution(mesh):
    return jax.shard_map(
        functools.partial(body, mesh.shape["pipe"], mesh.shape["ctx"]),
        mesh=mesh,
        in_specs=(
            P("pipe", "ctx", None),
            P("pipe", "ctx", None),
            P(("pipe", "ctx"), None),
            P(("pipe", "ctx"), None),
            P(),
        ),
        out_specs=P("pipe", "ctx", None),
        check_vma=False,
    )
```
